32 devices in a mesh: dp: 16 (over z, x, core), tensor: 2 (over y).
Axes of the slice: x: 2, y: 2, z: 4, core: 2. Of those that a mesh axis runs over, the one named last changes fastest.
Arguments:
- inputs: bfloat16 [6272, 512], P('dp'), may hold values from -6 to 6
- ln1_gain: float32 [512], replicated, may hold values from 0.5 to 1.5
- ln1_shift: float32 [512], replicated, may hold values from -3 to 3
- w_qkv: bfloat16 [512, 3, 512], P(None, None, 'tensor'), may hold values from -0.25 to 0.25
- qv_bias: float32 [2, 512], P(None, 'tensor'), may hold values from -3 to 3
- bias_table: float32 [169, 16], P(None, 'tensor'), may hold values from -6 to 320
- rel_index: int32 [49, 49], replicated, may hold values from 0 to 168
- regions: int32 [196], replicated, may hold values from 0 to 8
- w_proj: bfloat16 [512, 512], P('tensor'), may hold values from -0.5 to 0.5
- proj_bias: float32 [512], replicated, may hold values from -3 to 3
- ln2_gain: float32 [512], replicated, may hold values from 0.5 to 1.5
- ln2_shift: float32 [512], replicated, may hold values from -3 to 3
- w_fc1: bfloat16 [512, 2048], P(None, 'tensor'), may hold values from -0.25 to 0.25
- fc1_bias: float32 [2048], P('tensor'), may hold values from -3 to 3
- w_fc2: bfloat16 [2048, 512], P('tensor'), may hold values from -0.1875 to 0.1875
- fc2_bias: float32 [512], replicated, may hold values from -3 to 3
- grad_output: bfloat16 [6272, 512], P('dp'), may hold values from -12 to 12
Outputs:
- output: bfloat16 [6272, 512], P('dp')
- grad_input: float32 [6272, 512], P('dp')
- grad_ln1_gain: float32 [512], replicated
- grad_ln1_shift: float32 [512], replicated
- grad_qkv: float32 [512, 3, 512], P(None, None, 'tensor')
- grad_qv_bias: float32 [2, 512], P(None, 'tensor')
- grad_table: float32 [169, 16], P(None, 'tensor')
- grad_proj: float32 [512, 512], P('tensor')
- grad_proj_bias: float32 [512], replicated
- grad_ln2_gain: float32 [512], replicated
- grad_ln2_shift: float32 [512], replicated
- grad_fc1: float32 [512, 2048], P(None, 'tensor')
- grad_fc1_bias: float32 [2048], P('tensor')
- grad_fc2: float32 [2048, 512], P('tensor')
- grad_fc2_bias: float32 [512], replicated
The draws below stay inside these ranges and needn't reach their ends.
All inputs are finite; a program needn't handle non-finite values.
Results may differ from the reference program's by a relative error of at most 0.017.
Values may be sent and summed in bfloat16 or wider, within the bound.
No kernel may reach another device: no remote copies, remote signals or barrier semaphores. Data moves between devices by JAX's collectives and lax.ppermute only.
A program may use at most 64 MiB of HBM per device.

```python
import math
import jax
import jax.numpy as jnp
from jax import lax

D = 512
HEADS = 16
HEAD_DIM = 32
FF = 2048
SIDE = 14
WIN = 7
SHIFT = 3
REGIONS = 9
IMAGES = 32
TOKENS = 6272
TABLE = 169
N_TENSOR = 2


def draw_bias_table(key, part):
    base_table = jnp.clip(jax.random.normal(jax.random.fold_in(key, 11), (TABLE, HEADS), jnp.float32), -6.0, 6.0)
    return base_table


def draw_grad_output(key, part):
    ramp = 0.6 + 1.2 * jnp.arange(TOKENS, dtype=jnp.float32)[:, None] / max(TOKENS - 1, 1)
    noise = jnp.clip(jax.random.normal(jax.random.fold_in(key, 21), (TOKENS, D), jnp.float32), -6.0, 6.0)
    return jnp.clip(noise * ramp, -12.0, 12.0).astype(jnp.bfloat16)


def touch_ends(values, key, least, top_value):
    longest = values.shape.index(max(values.shape))
    spots = []
    for shift in (0, 1):
        where = [jax.random.randint(jax.random.fold_in(key, axis), (), 0, length) for axis, length in enumerate(values.shape)]
        where[longest] = (where[longest] + shift) % values.shape[longest]
        spots.append(tuple(where))
    return values.at[spots[0]].set(least).at[spots[1]].set(top_value)


def steps_of(key, shape, shards, smallest, top_value):
    factor_of = 1.0
    for dim, parts in shards:
        heights = jax.random.uniform(jax.random.fold_in(jax.random.fold_in(key, 6), dim), (parts,), jnp.float32, smallest / len(shards), top_value / len(shards))
        factor_of = factor_of * jnp.repeat(jnp.exp(heights), shape[dim] // parts).reshape((-1,) + (1,) * (len(shape) - 1 - dim))
    return factor_of


def bell_draw(own_key, extent, deviation, most, cuts=(), held_as=jnp.bfloat16):
    level = steps_of(own_key, extent, cuts, -0.22, 0.18) if cuts else 1.0
    drawn = jax.random.normal(own_key, extent, jnp.float32) * deviation * level
    return jnp.minimum(jnp.maximum(drawn, -most), most).astype(held_as)


def setup_inputs(seed: int = 0) -> dict:
    splits = jax.random.split(jax.random.key(seed), 18)
    inputs = bell_draw(splits[0], (TOKENS, D), 1.0, 6.0, ((0, 16),))
    ln1_gain = jnp.clip(1.0 + 0.1 * jax.random.normal(splits[1], (D,), jnp.float32), 0.5, 1.5)
    ln1_shift = bell_draw(splits[2], (D,), 0.5, 3.0, (), jnp.float32)
    w_qkv = bell_draw(splits[3], (D, 3, D), D ** -0.5, 0.25, ((2, 2),))
    qv_bias = bell_draw(splits[4], (2, D), 0.5, 3.0, ((1, 2),), jnp.float32)
    bias_table = draw_bias_table(jax.random.fold_in(splits[17], 71), 0)
    rel_index = touch_ends(jax.random.randint(splits[6], (WIN * WIN, WIN * WIN), 0, TABLE), jax.random.fold_in(splits[6], 1), 0, TABLE - 1).astype(jnp.int32)
    regions = touch_ends(jax.random.randint(splits[7], (SIDE * SIDE,), 0, REGIONS), jax.random.fold_in(splits[7], 1), 0, REGIONS - 1).astype(jnp.int32)
    w_proj = bell_draw(splits[8], (D, D), (D // 4) ** -0.5, 0.5, ((0, 2),))
    proj_bias = bell_draw(splits[9], (D,), 0.5, 3.0, (), jnp.float32)
    ln2_gain = jnp.clip(1.0 + 0.1 * jax.random.normal(splits[10], (D,), jnp.float32), 0.5, 1.5)
    ln2_shift = bell_draw(splits[11], (D,), 0.5, 3.0, (), jnp.float32)
    w_fc1 = bell_draw(splits[12], (D, FF), D ** -0.5, 0.25, ((1, 2),))
    fc1_bias = bell_draw(splits[13], (FF,), 0.5, 3.0, ((0, 2),), jnp.float32)
    w_fc2 = bell_draw(splits[14], (FF, D), (FF // 2) ** -0.5, 0.1875, ((0, 2),))
    fc2_bias = bell_draw(splits[15], (D,), 0.5, 3.0, (), jnp.float32)
    grad_output = draw_grad_output(jax.random.fold_in(splits[17], 71), 0)
    return {"inputs": inputs, "ln1_gain": ln1_gain, "ln1_shift": ln1_shift, "w_qkv": w_qkv, "qv_bias": qv_bias, "bias_table": bias_table, "rel_index": rel_index, "regions": regions, "w_proj": w_proj, "proj_bias": proj_bias, "ln2_gain": ln2_gain, "ln2_shift": ln2_shift, "w_fc1": w_fc1, "fc1_bias": fc1_bias, "w_fc2": w_fc2, "fc2_bias": fc2_bias, "grad_output": grad_output}


NORM_EPS = 1e-05
MASKED = -1e+30

def layer_norm(values, norm_gain, norm_shift):
    centered = values - lax.optimization_barrier(jnp.mean(values, axis=-1, keepdims=True))
    inverse = lax.rsqrt(lax.optimization_barrier(jnp.mean(centered * centered, axis=-1, keepdims=True)) + NORM_EPS)
    normed = centered * inverse
    return (normed * norm_gain + norm_shift, normed, inverse)

def norm_backward(upstream, normed, inverse, norm_gain):
    weighted = upstream * norm_gain
    return inverse * (weighted - lax.optimization_barrier(jnp.mean(weighted, axis=-1, keepdims=True)) - normed * lax.optimization_barrier(jnp.mean(weighted * normed, axis=-1, keepdims=True)))

def gelu_exact(hidden):
    return 0.5 * hidden * (1.0 + jax.scipy.special.erf(hidden * 0.7071067811865476))

def gelu_slope(hidden):
    return 0.5 * (1.0 + jax.scipy.special.erf(hidden * 0.7071067811865476)) + hidden * jnp.exp(-0.5 * hidden * hidden) * 0.3989422804014327

def to_windows(tensor, images):
    heads_here = tensor.shape[1]
    head_depth = tensor.shape[2]
    across = SIDE // WIN
    layout = tensor.reshape(images, SIDE, SIDE, heads_here, head_depth)
    layout = jnp.roll(layout, (-SHIFT, -SHIFT), axis=(1, 2))
    layout = layout.reshape(images, across, WIN, across, WIN, heads_here, head_depth).transpose(0, 1, 3, 5, 2, 4, 6)
    return layout.reshape(images * across * across, heads_here, WIN * WIN, head_depth)

def from_windows(tensor, images):
    heads_here = tensor.shape[1]
    head_depth = tensor.shape[3]
    across = SIDE // WIN
    layout = tensor.reshape(images, across, across, heads_here, WIN, WIN, head_depth).transpose(0, 1, 4, 2, 5, 3, 6)
    layout = jnp.roll(layout.reshape(images, SIDE, SIDE, heads_here, head_depth), (SHIFT, SHIFT), axis=(1, 2))
    return layout.reshape(images * SIDE * SIDE, heads_here * head_depth)

def window_scores(queries, keys_win, rel_bias, allowed, images):
    raw_scores = jnp.einsum('whie,whje->whij', queries.astype(jnp.float32), keys_win.astype(jnp.float32))
    layout = raw_scores.reshape((images, allowed.shape[0]) + raw_scores.shape[1:]) + rel_bias[None, None]
    return jnp.where(allowed[None, :, None], layout, MASKED)

def round_sum(partial_value):
    rounded = lax.optimization_barrier(partial_value.astype(jnp.bfloat16))
    return lax.optimization_barrier(jnp.sum(rounded.astype(jnp.float32), axis=0))

def tensor_sum(left, right):
    block_rows, inner = left.shape
    per_group = inner // N_TENSOR
    pieces = left.reshape(block_rows, N_TENSOR, per_group).astype(jnp.float32)
    weights = right.reshape(N_TENSOR, per_group, right.shape[1]).astype(jnp.float32)
    return round_sum(jnp.einsum('tnc,ncd->ntd', pieces, weights))

def qkv_sum(grad_three, weight):
    block_rows = grad_three.shape[0]
    per_group = weight.shape[2] // N_TENSOR
    left = grad_three.reshape(block_rows, 3, N_TENSOR, per_group).astype(jnp.float32)
    right = weight.reshape(weight.shape[0], 3, N_TENSOR, per_group).astype(jnp.float32)
    return round_sum(jnp.einsum('tkgc,dkgc->gtd', left, right))

def block_pass(block_in, block_grad, params):
    ln1_gain, ln1_shift, w_qkv, qv_bias, bias_table, rel_index, regions, w_proj, proj_bias, ln2_gain, ln2_shift, w_fc1, fc1_bias, w_fc2, fc2_bias = params
    tokens_here = block_in.shape[0]
    images = tokens_here // (SIDE * SIDE)
    q_factor = HEAD_DIM ** (-0.5)
    across = SIDE // WIN
    residual_in = block_in.astype(jnp.float32)
    normed_one, unit_one, inverse_one = layer_norm(residual_in, ln1_gain, ln1_shift)
    normed_one_b = normed_one.astype(jnp.bfloat16)
    qkv_weight = w_qkv.reshape(D, 3 * D)
    projected = jnp.dot(normed_one_b, qkv_weight, preferred_element_type=jnp.float32).reshape(tokens_here, 3, D)
    queries = ((projected[:, 0] + qv_bias[0]) * q_factor).astype(jnp.bfloat16)
    keys_tok = projected[:, 1].astype(jnp.bfloat16)
    values_tok = (projected[:, 2] + qv_bias[1]).astype(jnp.bfloat16)
    query_win = to_windows(queries.reshape(tokens_here, HEADS, HEAD_DIM), images)
    key_win = to_windows(keys_tok.reshape(tokens_here, HEADS, HEAD_DIM), images)
    value_win = to_windows(values_tok.reshape(tokens_here, HEADS, HEAD_DIM), images)
    region_win = regions.reshape(across, WIN, across, WIN).transpose(0, 2, 1, 3).reshape(across * across, WIN * WIN)
    allowed = region_win[:, :, None] == region_win[:, None, :]
    rel_bias = bias_table[rel_index.reshape(-1)].T.reshape(HEADS, WIN * WIN, WIN * WIN)
    scores = window_scores(query_win, key_win, rel_bias, allowed, images)
    top_score = lax.optimization_barrier(jnp.max(scores, axis=-1, keepdims=True))
    log_total = top_score + jnp.log(lax.optimization_barrier(jnp.sum(jnp.exp(scores - top_score), axis=-1, keepdims=True)))
    prob = jnp.exp(scores - log_total)
    prob_b = prob.astype(jnp.bfloat16).reshape(-1, HEADS, WIN * WIN, WIN * WIN)
    mixed = jnp.einsum('whij,whje->whie', prob_b.astype(jnp.float32), value_win.astype(jnp.float32))
    mixed_tok = from_windows(mixed.astype(jnp.bfloat16), images)
    attn_total = tensor_sum(mixed_tok, w_proj)
    hidden_res = residual_in + attn_total + proj_bias
    normed_two, unit_two, inverse_two = layer_norm(hidden_res, ln2_gain, ln2_shift)
    normed_two_b = normed_two.astype(jnp.bfloat16)
    pre_act = jnp.dot(normed_two_b, w_fc1, preferred_element_type=jnp.float32) + fc1_bias
    activ_b = gelu_exact(pre_act).astype(jnp.bfloat16)
    mlp_total = tensor_sum(activ_b, w_fc2)
    result = (hidden_res + mlp_total + fc2_bias).astype(jnp.bfloat16)
    upstream = block_grad.astype(jnp.float32)
    grad_fc2_bias = lax.optimization_barrier(jnp.sum(upstream, axis=0))
    grad_fc2 = jnp.dot(activ_b.T, block_grad, preferred_element_type=jnp.float32)
    grad_act = jnp.dot(block_grad, w_fc2.T, preferred_element_type=jnp.float32)
    grad_pre = grad_act * gelu_slope(pre_act)
    grad_pre_b = grad_pre.astype(jnp.bfloat16)
    grad_fc1_bias = lax.optimization_barrier(jnp.sum(grad_pre, axis=0))
    grad_fc1 = jnp.dot(normed_two_b.T, grad_pre_b, preferred_element_type=jnp.float32)
    back_two = tensor_sum(grad_pre_b, w_fc1.T)
    grad_ln2_gain = lax.optimization_barrier(jnp.sum(back_two * unit_two, axis=0))
    grad_ln2_shift = lax.optimization_barrier(jnp.sum(back_two, axis=0))
    grad_hidden = upstream + norm_backward(back_two, unit_two, inverse_two, ln2_gain)
    grad_hidden_b = grad_hidden.astype(jnp.bfloat16)
    grad_proj_bias = lax.optimization_barrier(jnp.sum(grad_hidden, axis=0))
    grad_proj = jnp.dot(mixed_tok.T, grad_hidden_b, preferred_element_type=jnp.float32)
    grad_mixed = jnp.dot(grad_hidden_b, w_proj.T, preferred_element_type=jnp.float32).astype(jnp.bfloat16)
    grad_mixed_win = to_windows(grad_mixed.reshape(tokens_here, HEADS, HEAD_DIM), images)
    scores_again = window_scores(query_win, key_win, rel_bias, allowed, images)
    prob_again = jnp.exp(scores_again - log_total)
    prob_again_b = prob_again.astype(jnp.bfloat16).reshape(-1, HEADS, WIN * WIN, WIN * WIN)
    grad_prob = jnp.einsum('whie,whje->whij', grad_mixed_win.astype(jnp.float32), value_win.astype(jnp.float32)).reshape(prob_again.shape)
    row_dot = lax.optimization_barrier(jnp.sum(prob_again * grad_prob, axis=-1, keepdims=True))
    grad_score = prob_again * (grad_prob - row_dot)
    summed_scores = lax.optimization_barrier(jnp.sum(grad_score, axis=(0, 1))).reshape(HEADS, WIN * WIN * WIN * WIN)
    grad_table = jax.ops.segment_sum(summed_scores.T, rel_index.reshape(-1), num_segments=TABLE)
    grad_score_b = grad_score.astype(jnp.bfloat16).reshape(-1, HEADS, WIN * WIN, WIN * WIN).astype(jnp.float32)
    grad_query_win = jnp.einsum('whij,whje->whie', grad_score_b, key_win.astype(jnp.float32)) * q_factor
    grad_key_win = jnp.einsum('whij,whie->whje', grad_score_b, query_win.astype(jnp.float32))
    grad_value_win = jnp.einsum('whij,whie->whje', prob_again_b.astype(jnp.float32), grad_mixed_win.astype(jnp.float32))
    grad_query = from_windows(grad_query_win, images)
    grad_key = from_windows(grad_key_win, images)
    grad_value = from_windows(grad_value_win, images)
    grad_qv_bias = jnp.stack([lax.optimization_barrier(jnp.sum(grad_query, axis=0)), lax.optimization_barrier(jnp.sum(grad_value, axis=0))])
    grad_three = jnp.stack([grad_query, grad_key, grad_value], axis=1).astype(jnp.bfloat16)
    grad_qkv = jnp.dot(normed_one_b.T, grad_three.reshape(tokens_here, 3 * D), preferred_element_type=jnp.float32).reshape(D, 3, D)
    back_one = qkv_sum(grad_three, w_qkv)
    grad_ln1_gain = lax.optimization_barrier(jnp.sum(back_one * unit_one, axis=0))
    grad_ln1_shift = lax.optimization_barrier(jnp.sum(back_one, axis=0))
    grad_in = grad_hidden + norm_backward(back_one, unit_one, inverse_one, ln1_gain)
    grads = (grad_ln1_gain, grad_ln1_shift, grad_qkv, grad_qv_bias, grad_table, grad_proj, grad_proj_bias, grad_ln2_gain, grad_ln2_shift, grad_fc1, grad_fc1_bias, grad_fc2, grad_fc2_bias)
    return (result, grad_in, grads)

def reference(inputs, ln1_gain, ln1_shift, w_qkv, qv_bias, bias_table, rel_index, regions, w_proj, proj_bias, ln2_gain, ln2_shift, w_fc1, fc1_bias, w_fc2, fc2_bias, grad_output):
    params = (ln1_gain, ln1_shift, w_qkv, qv_bias, bias_table, rel_index, regions, w_proj, proj_bias, ln2_gain, ln2_shift, w_fc1, fc1_bias, w_fc2, fc2_bias)
    per_block = math.gcd(IMAGES, 16)
    blocks = IMAGES // per_block
    block_rows = per_block * SIDE * SIDE
    stacked_in = inputs.reshape(blocks, block_rows, D)
    stacked_grad = grad_output.reshape(blocks, block_rows, D)

    def one_block(carry, block_pair):
        result, grad_in, grads = block_pass(block_pair[0], block_pair[1], params)
        return (tuple((left + right for left, right in zip(carry, grads))), (result, grad_in))
    initial = (jnp.zeros((D,), jnp.float32), jnp.zeros((D,), jnp.float32), jnp.zeros((D, 3, D), jnp.float32), jnp.zeros((2, D), jnp.float32), jnp.zeros((TABLE, HEADS), jnp.float32), jnp.zeros((D, D), jnp.float32), jnp.zeros((D,), jnp.float32), jnp.zeros((D,), jnp.float32), jnp.zeros((D,), jnp.float32), jnp.zeros((D, FF), jnp.float32), jnp.zeros((FF,), jnp.float32), jnp.zeros((FF, D), jnp.float32), jnp.zeros((D,), jnp.float32))
    totals, (results, grads_in) = lax.scan(one_block, initial, (stacked_in, stacked_grad))
    return (results.reshape(TOKENS, D), grads_in.reshape(TOKENS, D), totals[0], totals[1], totals[2], totals[3], totals[4], totals[5], totals[6], totals[7], totals[8], totals[9], totals[10], totals[11], totals[12])
```

```python
import functools

import numpy as np
import jax
import jax.numpy as jnp
from jax import lax
from jax.experimental import pallas as pl
from jax.experimental.pallas import tpu as pltpu
from jax.sharding import PartitionSpec as P

HEAD_DIM = 32
SIDE = 14
WIN = 7
SHIFT = 3
ACROSS = SIDE // WIN
POSITIONS = WIN * WIN
PAD = 64
WINDOWS = ACROSS * ACROSS

NORM_EPS = 1e-05
MASKED = -1e30
F32 = jnp.float32
BF16 = jnp.bfloat16
HIDDEN_BLOCK = 256


def dot(a, b, dims=((1,), (0,)), precision=None):
    return lax.dot_general(a, b, (dims, ((), ())), preferred_element_type=F32, precision=precision)


NN = ((1,), (0,))
NT = ((1,), (1,))
TN = ((0,), (0,))


def normed(values):
    centered = values - jnp.mean(values, axis=-1, keepdims=True)
    inverse = lax.rsqrt(jnp.mean(centered * centered, axis=-1, keepdims=True) + NORM_EPS)
    return centered * inverse, inverse


def norm_backward(upstream, unit, inverse, gain):
    weighted = upstream * gain
    return inverse * (
        weighted
        - jnp.mean(weighted, axis=-1, keepdims=True)
        - unit * jnp.mean(weighted * unit, axis=-1, keepdims=True)
    )


def window_order():
    order = np.zeros((WINDOWS * PAD, SIDE * SIDE), np.float32)
    for a in range(ACROSS):
        for b in range(ACROSS):
            for i in range(POSITIONS):
                row = (a * WIN + i // WIN + SHIFT) % SIDE
                col = (b * WIN + i % WIN + SHIFT) % SIDE
                order[(a * ACROSS + b) * PAD + i, row * SIDE + col] = 1.0
    return order


def spread_heads(tile, mask):
    heads = mask.shape[0] // tile.shape[0]
    return jnp.concatenate([tile] * heads, axis=0) * mask


def gather_heads(full, mask, heads):
    total = None
    for h in range(heads):
        rows = slice(h * PAD, (h + 1) * PAD)
        part = full[rows, :] * mask[rows, :].astype(F32)
        total = part if total is None else total + part
    return total


def attn_forward_kernel(
    x_ref, gain_ref, shift_ref, wqkv_ref, qvb_ref, table_ref, rel_ref, creg_ref, rreg_ref,
    perm_ref, hmask_ref, wproj_ref,
    part_ref, n1_ref, qkvw_ref, prob_ref, otok_ref,
    bm_ref, ow_ref,
):
    inner = wproj_ref.shape[0]
    heads = inner // HEAD_DIM
    lanes = heads * PAD
    unit, _ = normed(x_ref[...].astype(F32))
    n1 = (unit * gain_ref[...] + shift_ref[...]).astype(BF16)
    n1_ref[...] = n1
    proj = dot(n1, wqkv_ref[...])
    q = ((proj[:, :inner] + qvb_ref[0:1, :]) * (HEAD_DIM ** (-0.5))).astype(BF16)
    k = proj[:, inner : 2 * inner].astype(BF16)
    v = (proj[:, 2 * inner :] + qvb_ref[1:2, :]).astype(BF16)
    perm = perm_ref[...]
    qkvw_ref[:, :inner] = dot(perm, q).astype(BF16)
    qkvw_ref[:, inner : 2 * inner] = dot(perm, k).astype(BF16)
    qkvw_ref[:, 2 * inner :] = dot(perm, v).astype(BF16)

    rel = rel_ref[...]
    pairs = lanes // rel.shape[1]
    width = rel.shape[1]

    def pick(t, acc):
        hit = rel == t
        row = table_ref[pl.ds(t, 1), :]
        return tuple(
            jnp.where(hit, row[:, p * width : (p + 1) * width], acc[p]) for p in range(pairs)
        )

    zero = jnp.zeros(rel.shape, F32)
    picked = lax.fori_loop(0, table_ref.shape[0], pick, (zero,) * pairs)
    bias = jnp.concatenate(picked, axis=1)
    for w in range(WINDOWS):
        hit = creg_ref[:, w : w + 1] == rreg_ref[w : w + 1, :]
        bm_ref[w * PAD : (w + 1) * PAD, :] = jnp.where(hit, bias, MASKED)

    def window(i, carry):
        rows = pl.ds(pl.multiple_of(i * PAD, PAD), PAD)
        hmask = hmask_ref[...]
        qw = qkvw_ref[rows, :inner]
        kw = qkvw_ref[rows, inner : 2 * inner]
        vw = qkvw_ref[rows, 2 * inner :]
        brows = pl.ds(pl.multiple_of(lax.rem(i, WINDOWS) * PAD, PAD), PAD)
        s = dot(kw, spread_heads(qw, hmask), NT) + bm_ref[brows, :]
        e = jnp.exp(s - jnp.max(s, axis=0, keepdims=True))
        p = e * (1.0 / jnp.sum(e, axis=0, keepdims=True))
        prob_ref[rows, :] = p
        full = dot(p.astype(BF16), vw, TN)
        ow_ref[rows, :] = gather_heads(full, hmask, heads).astype(BF16)
        return carry

    lax.fori_loop(0, qkvw_ref.shape[0] // PAD, window, 0)
    otok = dot(perm, ow_ref[...], TN).astype(BF16)
    otok_ref[...] = otok
    part_ref[...] = dot(otok, wproj_ref[...]).astype(BF16)


def mlp_kernel(
    x_ref, own_ref, recv_ref, pbias_ref, gain_ref, shift_ref, w1_ref, b1_ref, w2_ref, dy_ref,
    back_ref, h1_ref, n2_ref, act_ref, dub_ref, gb1_ref, gb2_ref,
    acc_ref,
):
    step = pl.program_id(0)

    @pl.when(step == 0)
    def _():
        h1 = (
            x_ref[...].astype(F32)
            + (own_ref[...].astype(F32) + recv_ref[...].astype(F32))
            + pbias_ref[...]
        )
        h1_ref[...] = h1
        unit, _ = normed(h1)
        n2_ref[...] = (unit * gain_ref[...] + shift_ref[...]).astype(BF16)
        gb2_ref[...] = jnp.sum(dy_ref[...].astype(F32), axis=0, keepdims=True)
        acc_ref[...] = jnp.zeros_like(acc_ref)

    u = dot(n2_ref[...], w1_ref[...]) + b1_ref[...]
    cdf = 0.5 * (1.0 + lax.erf(u * 0.7071067811865476))
    act_ref[...] = (u * cdf).astype(BF16)
    slope = cdf + u * jnp.exp(-0.5 * u * u) * 0.3989422804014327
    du = dot(dy_ref[...], w2_ref[...], NT) * slope
    gb1_ref[...] = jnp.sum(du, axis=0, keepdims=True)
    dub = du.astype(BF16)
    dub_ref[...] = dub
    acc_ref[...] += dot(dub, w1_ref[...], NT)

    @pl.when(step == pl.num_programs(0) - 1)
    def _():
        back_ref[...] = acc_ref[...].astype(BF16)


def half(ref, which, size):
    return ref[:, pl.ds(pl.multiple_of(which * size, size), size)]


def mlp_grad_kernel(bit_ref, act_ref, dub_ref, n2_ref, dy_ref, w2_ref, keep_ref, send_ref, part_ref):
    bit = bit_ref[0]
    size = act_ref.shape[1] // 2
    for out, which in ((send_ref, 1 - bit), (keep_ref, bit)):
        out[:size, :] = dot(half(act_ref, which, size), dy_ref[...], TN).astype(BF16)
        out[size:, :] = dot(n2_ref[...], half(dub_ref, which, size), TN).astype(BF16)
    part_ref[...] = dot(act_ref[...], w2_ref[...]).astype(BF16)


def attn_backward_kernel(
    dy_ref, own_ref, recv_ref, h1_ref, gain_ref, wproj_ref, qkvw_ref, prob_ref, perm_ref,
    hmask_ref, wqkv_ref,
    part_ref, dh_ref, dhb_ref, dp_ref, sums_ref, dsum_ref,
    dow_ref, dqkv_ref,
):
    inner = wproj_ref.shape[0]
    heads = inner // HEAD_DIM
    dn2 = own_ref[...].astype(F32) + recv_ref[...].astype(F32)
    unit, inverse = normed(h1_ref[...])
    sums_ref[0:1, :] = jnp.sum(dn2 * unit, axis=0, keepdims=True)
    sums_ref[1:2, :] = jnp.sum(dn2, axis=0, keepdims=True)
    dh = dy_ref[...].astype(F32) + norm_backward(dn2, unit, inverse, gain_ref[...])
    dh_ref[...] = dh
    sums_ref[2:3, :] = jnp.sum(dh, axis=0, keepdims=True)
    dhb = dh.astype(BF16)
    dhb_ref[...] = dhb
    perm = perm_ref[...]
    dow_ref[...] = dot(perm, dot(dhb, wproj_ref[...], NT).astype(BF16)).astype(BF16)
    dsum_ref[...] = jnp.zeros_like(dsum_ref)

    def window(i, carry):
        qsum, vsum = carry
        rows = pl.ds(pl.multiple_of(i * PAD, PAD), PAD)
        hmask = hmask_ref[...]
        qblk = spread_heads(qkvw_ref[rows, :inner], hmask)
        kw = qkvw_ref[rows, inner : 2 * inner]
        vw = qkvw_ref[rows, 2 * inner :]
        oblk = spread_heads(dow_ref[rows, :], hmask)
        p = prob_ref[rows, :]
        dp = dot(vw, oblk, NT)
        ds = p * (dp - jnp.sum(p * dp, axis=0, keepdims=True))
        dsum_ref[...] += ds
        dsb = ds.astype(BF16)
        dq = gather_heads(dot(dsb, kw, TN), hmask, heads) * (HEAD_DIM ** (-0.5))
        dk = dot(dsb, qblk)
        dv = dot(p.astype(BF16), oblk)
        dqkv_ref[rows, :inner] = dq.astype(BF16)
        dqkv_ref[rows, inner : 2 * inner] = dk.astype(BF16)
        dqkv_ref[rows, 2 * inner :] = dv.astype(BF16)
        return (
            qsum + jnp.sum(dq, axis=0, keepdims=True),
            vsum + jnp.sum(dv, axis=0, keepdims=True),
        )

    zero = jnp.zeros((1, inner), F32)
    qsum, vsum = lax.fori_loop(0, qkvw_ref.shape[0] // PAD, window, (zero, zero))
    sums_ref[3:4, :inner] = qsum
    sums_ref[3:4, inner:] = vsum
    dp_tok = dot(perm, dqkv_ref[...], TN).astype(BF16)
    dp_ref[...] = dp_tok
    part_ref[...] = dot(dp_tok, wqkv_ref[...], NT).astype(BF16)


def attn_grad_kernel(bit_ref, n1_ref, dp_ref, otok_ref, dhb_ref, keep_ref, send_ref):
    bit = bit_ref[0]
    wide = dp_ref.shape[1]
    rows = n1_ref.shape[1] // 2
    for out, which in ((send_ref, 1 - bit), (keep_ref, bit)):
        out[:, :wide] = dot(half(n1_ref, which, rows), dp_ref[...], TN).astype(BF16)
        out[:, wide:] = dot(otok_ref[...], half(dhb_ref, which, rows), TN).astype(BF16)


def table_kernel(dsum_ref, rel_ref, group_ref, out_ref, tab_ref):
    rel = rel_ref[...]
    width = rel.shape[1]
    pairs = dsum_ref.shape[1] // width

    def eight(n, carry):
        for p in range(pairs):
            cols = slice(p * width, (p + 1) * width)
            part = dsum_ref[:, cols]
            found = [
                jnp.sum(jnp.where(rel == n * 8 + t, part, 0.0), axis=0, keepdims=True)
                for t in range(8)
            ]
            tab_ref[pl.ds(pl.multiple_of(n * 8, 8), 8), cols] = jnp.concatenate(found, axis=0)
        return carry

    lax.fori_loop(0, tab_ref.shape[0] // 8, eight, 0)
    out_ref[...] = dot(group_ref[...], tab_ref[...], NT, lax.Precision.HIGHEST)


def input_grad_kernel(x_ref, own_ref, recv_ref, dh_ref, gain_ref, gin_ref, sums_ref):
    unit, inverse = normed(x_ref[...].astype(F32))
    dn1 = own_ref[...].astype(F32) + recv_ref[...].astype(F32)
    sums_ref[0:1, :] = jnp.sum(dn1 * unit, axis=0, keepdims=True)
    sums_ref[1:2, :] = jnp.sum(dn1, axis=0, keepdims=True)
    gin_ref[...] = dh_ref[...] + norm_backward(dn1, unit, inverse, gain_ref[...])


def output_kernel(h1_ref, own_ref, recv_ref, bias_ref, out_ref):
    total = own_ref[...].astype(F32) + recv_ref[...].astype(F32)
    out_ref[...] = (h1_ref[...] + total + bias_ref[...]).astype(BF16)


def shape(dims, dtype):
    return jax.ShapeDtypeStruct(dims, dtype)


VMEM = functools.partial(pl.BlockSpec, memory_space=pltpu.VMEM)
SMEM = functools.partial(pl.BlockSpec, memory_space=pltpu.SMEM)


def swap(value, axis, size, bit):
    return lax.ppermute(value, axis, [(i, i ^ bit) for i in range(size)])


def add_pair(left, right):
    return left.astype(F32) + right.astype(F32)


def reduce_scatter(keep, send, bits, size):
    index = lax.axis_index("dp")
    for n, bit in enumerate(bits):
        keep = add_pair(keep, swap(send, "dp", size, bit)).astype(BF16)
        if n + 1 < len(bits):
            rows = keep.shape[0] // 2
            low, high = keep[:rows], keep[rows:]
            upper = (index & bits[n + 1]) != 0
            keep, send = jnp.where(upper, high, low), jnp.where(upper, low, high)
    return keep


def gather_back(value, bits, size):
    index = lax.axis_index("dp")
    for bit in reversed(bits[1:]):
        other = swap(value, "dp", size, bit)
        upper = (index & bit) != 0
        value = jnp.concatenate(
            [jnp.where(upper, other, value), jnp.where(upper, value, other)], axis=0
        )
    other = swap(value, "dp", size, bits[0])
    upper = (index & bits[0]) != 0
    return jnp.where(upper, other, value), jnp.where(upper, value, other)


def local(
    dp_size,
    inputs,
    ln1_gain,
    ln1_shift,
    w_qkv,
    qv_bias,
    bias_table,
    rel_index,
    regions,
    w_proj,
    proj_bias,
    ln2_gain,
    ln2_shift,
    w_fc1,
    fc1_bias,
    w_fc2,
    fc2_bias,
    grad_output,
):
    tokens, width = inputs.shape
    images = tokens // (SIDE * SIDE)
    inner = w_qkv.shape[2]
    heads = inner // HEAD_DIM
    lanes = heads * PAD
    wrows = images * WINDOWS * PAD
    hidden = w_fc1.shape[1]
    table_rows = bias_table.shape[0]
    table_pad = -(-table_rows // 8) * 8
    row = lambda v: v.reshape(1, -1)
    tensor_swap = lambda v: swap(v, "tensor", 2, 1)
    bits = [1 << n for n in range(dp_size.bit_length() - 1)]
    core_bit = (lax.axis_index("dp") & 1).astype(jnp.int32).reshape(1)

    perm = jnp.asarray(np.kron(np.eye(images, dtype=np.float32), window_order()), BF16)
    hmask = jnp.asarray(
        np.kron(np.eye(heads, dtype=np.float32), np.ones((PAD, HEAD_DIM), np.float32)), BF16
    )
    group = jnp.asarray(np.kron(np.eye(heads, dtype=np.float32), np.ones((1, PAD), np.float32)))
    rel = jnp.pad(rel_index.T, ((0, PAD - POSITIONS),) * 2, constant_values=-1)
    rel = jnp.concatenate([rel, rel], axis=1)
    region_win = (
        regions.reshape(ACROSS, WIN, ACROSS, WIN).transpose(0, 2, 1, 3).reshape(WINDOWS, POSITIONS)
    )
    pad = ((0, 0), (0, PAD - POSITIONS))
    creg = jnp.pad(region_win, pad, constant_values=-1).T
    rreg = jnp.tile(jnp.pad(region_win, pad, constant_values=-2), (1, heads))
    table = jnp.repeat(bias_table, PAD, axis=1)
    qkv_weight = w_qkv.reshape(width, 3 * inner)

    attn_part, n1, qkvw, prob, otok = pl.pallas_call(
        attn_forward_kernel,
        out_shape=(
            shape((tokens, width), BF16),
            shape((tokens, width), BF16),
            shape((wrows, 3 * inner), BF16),
            shape((wrows, lanes), F32),
            shape((tokens, inner), BF16),
        ),
        scratch_shapes=[
            pltpu.VMEM((WINDOWS * PAD, lanes), F32),
            pltpu.VMEM((wrows, inner), BF16),
        ],
        name="attn_forward",
    )(
        inputs, row(ln1_gain), row(ln1_shift), qkv_weight, qv_bias, table, rel, creg, rreg,
        perm, hmask, w_proj,
    )
    attn_recv = tensor_swap(attn_part)

    steps = hidden // HIDDEN_BLOCK
    full = lambda dims: pl.BlockSpec(dims, lambda j: (0, 0))
    cols = lambda rows: pl.BlockSpec((rows, HIDDEN_BLOCK), lambda j: (0, j))
    back_two_part, h1, n2, act, dub, grad_b1, grad_b2 = pl.pallas_call(
        mlp_kernel,
        grid=(steps,),
        in_specs=[
            full((tokens, width)), full((tokens, width)), full((tokens, width)), full((1, width)),
            full((1, width)), full((1, width)), cols(width), cols(1),
            pl.BlockSpec((HIDDEN_BLOCK, width), lambda j: (j, 0)), full((tokens, width)),
        ],
        out_specs=(
            full((tokens, width)), full((tokens, width)), full((tokens, width)), cols(tokens),
            cols(tokens), cols(1), full((1, width)),
        ),
        out_shape=(
            shape((tokens, width), BF16),
            shape((tokens, width), F32),
            shape((tokens, width), BF16),
            shape((tokens, hidden), BF16),
            shape((tokens, hidden), BF16),
            shape((1, hidden), F32),
            shape((1, width), F32),
        ),
        scratch_shapes=[pltpu.VMEM((tokens, width), F32)],
        name="mlp",
    )(
        inputs, attn_part, attn_recv, row(proj_bias), row(ln2_gain), row(ln2_shift), w_fc1,
        row(fc1_bias), w_fc2, grad_output,
    )
    back_two_recv = tensor_swap(back_two_part)

    keep, send, mlp_part = pl.pallas_call(
        mlp_grad_kernel,
        in_specs=[SMEM()] + [VMEM()] * 5,
        out_shape=(
            shape((hidden // 2 + width, width), BF16),
            shape((hidden // 2 + width, width), BF16),
            shape((tokens, width), BF16),
        ),
        cost_estimate=pl.CostEstimate(
            flops=6 * tokens * hidden * width, bytes_accessed=8 << 20, transcendentals=0
        ),
        name="mlp_grad",
    )(core_bit, act, dub, n2, grad_output, w_fc2)
    mlp_shard = reduce_scatter(keep, send, bits, dp_size)

    back_one_part, dh, dhb, dproj, sums, dsum = pl.pallas_call(
        attn_backward_kernel,
        out_shape=(
            shape((tokens, width), BF16),
            shape((tokens, width), F32),
            shape((tokens, width), BF16),
            shape((tokens, 3 * inner), BF16),
            shape((4, width), F32),
            shape((PAD, lanes), F32),
        ),
        scratch_shapes=[
            pltpu.VMEM((wrows, inner), BF16),
            pltpu.VMEM((wrows, 3 * inner), BF16),
        ],
        name="attn_backward",
    )(
        grad_output, back_two_part, back_two_recv, h1, row(ln2_gain), w_proj, qkvw, prob, perm,
        hmask, qkv_weight,
    )
    back_one_recv = tensor_swap(back_one_part)

    keep, send = pl.pallas_call(
        attn_grad_kernel,
        in_specs=[SMEM()] + [VMEM()] * 4,
        out_shape=(
            shape((width // 2, 3 * inner + inner), BF16),
            shape((width // 2, 3 * inner + inner), BF16),
        ),
        cost_estimate=pl.CostEstimate(
            flops=8 * tokens * inner * width, bytes_accessed=4 << 20, transcendentals=0
        ),
        name="attn_grad",
    )(core_bit, n1, dproj, otok, dhb)
    attn_shard = reduce_scatter(keep, send, bits, dp_size)

    table_sum = pl.pallas_call(
        table_kernel,
        out_shape=shape((heads, table_pad), F32),
        scratch_shapes=[pltpu.VMEM((table_pad, lanes), F32)],
        name="table",
    )(dsum, rel, group)

    mlp_recv = tensor_swap(mlp_part)
    output = pl.pallas_call(
        output_kernel, out_shape=shape((tokens, width), BF16), name="output"
    )(h1, mlp_part, mlp_recv, row(fc2_bias))

    grad_input, ln1_sums = pl.pallas_call(
        input_grad_kernel,
        out_shape=(shape((tokens, width), F32), shape((2, width), F32)),
        name="input_grad",
    )(inputs, back_one_part, back_one_recv, dh, row(ln1_gain))

    small = jnp.concatenate(
        [
            sums.reshape(-1),
            ln1_sums.reshape(-1),
            grad_b2.reshape(-1),
            grad_b1.reshape(-1),
            table_sum.reshape(-1),
        ]
    )
    for bit in bits:
        small = small + swap(small, "dp", dp_size, bit)
    s = small[: 4 * width].reshape(4, width)
    rest = small[4 * width :]
    grad_ln1_gain, grad_ln1_shift, grad_fc2_bias = rest[: 3 * width].reshape(3, width)
    grad_fc1_bias = rest[3 * width : 3 * width + hidden]
    grad_table = rest[3 * width + hidden :].reshape(heads, table_pad)[:, :table_rows].T
    grad_qv_bias = s[3].reshape(2, inner)

    low, high = gather_back(mlp_shard, bits, dp_size)
    mid = hidden // 2
    grad_fc2 = jnp.concatenate([low[:mid], high[:mid]], axis=0).astype(F32)
    grad_fc1 = jnp.concatenate([low[mid:], high[mid:]], axis=1).astype(F32)
    low, high = gather_back(attn_shard, bits, dp_size)
    grad_qkv = (
        jnp.concatenate([low[:, : 3 * inner], high[:, : 3 * inner]], axis=0)
        .astype(F32)
        .reshape(width, 3, inner)
    )
    grad_proj = jnp.concatenate([low[:, 3 * inner :], high[:, 3 * inner :]], axis=1).astype(F32)

    return (
        output, grad_input, grad_ln1_gain, grad_ln1_shift, grad_qkv, grad_qv_bias, grad_table,
        grad_proj, s[2], s[0], s[1], grad_fc1, grad_fc1_bias, grad_fc2, grad_fc2_bias,
    )


def solution(mesh):
    return jax.shard_map(
        functools.partial(local, mesh.shape["dp"]),
        mesh=mesh,
        in_specs=(
            P("dp", None),
            P(),
            P(),
            P(None, None, "tensor"),
            P(None, "tensor"),
            P(None, "tensor"),
            P(),
            P(),
            P("tensor", None),
            P(),
            P(),
            P(),
            P(None, "tensor"),
            P("tensor"),
            P("tensor", None),
            P(),
            P("dp", None),
        ),
        out_specs=(
            P("dp", None),
            P("dp", None),
            P(),
            P(),
            P(None, None, "tensor"),
            P(None, "tensor"),
            P(None, "tensor"),
            P("tensor", None),
            P(),
            P(),
            P(),
            P(None, "tensor"),
            P("tensor"),
            P("tensor", None),
            P(),
        ),
        check_vma=False,
    )
```

```python
import functools

import numpy as np
import jax
import jax.numpy as jnp
from jax import lax
from jax.experimental import pallas as pl
from jax.experimental.pallas import tpu as pltpu
from jax.sharding import PartitionSpec as P

HEAD_DIM = 32
SIDE = 14
WIN = 7
SHIFT = 3
ACROSS = SIDE // WIN
POSITIONS = WIN * WIN
PAD = 64
WINDOWS = ACROSS * ACROSS

NORM_EPS = 1e-05
MASKED = -1e30
F32 = jnp.float32
BF16 = jnp.bfloat16
HIDDEN_BLOCK = 256


def dot(a, b, dims=((1,), (0,)), precision=None):
    return lax.dot_general(a, b, (dims, ((), ())), preferred_element_type=F32, precision=precision)


NT = ((1,), (1,))
TN = ((0,), (0,))


def normed(values):
    centered = values - jnp.mean(values, axis=-1, keepdims=True)
    inverse = lax.rsqrt(jnp.mean(centered * centered, axis=-1, keepdims=True) + NORM_EPS)
    return centered * inverse, inverse


def norm_backward(upstream, unit, inverse, gain):
    weighted = upstream * gain
    return inverse * (
        weighted
        - jnp.mean(weighted, axis=-1, keepdims=True)
        - unit * jnp.mean(weighted * unit, axis=-1, keepdims=True)
    )


def window_order(shift=SHIFT):
    order = np.zeros((WINDOWS * PAD, SIDE * SIDE), np.float32)
    for a in range(ACROSS):
        for b in range(ACROSS):
            for i in range(POSITIONS):
                row = (a * WIN + i // WIN + shift) % SIDE
                col = (b * WIN + i % WIN + shift) % SIDE
                order[(a * ACROSS + b) * PAD + i, row * SIDE + col] = 1.0
    return order


def spread_heads(tile, mask):
    heads = mask.shape[0] // tile.shape[0]
    return jnp.concatenate([tile] * heads, axis=0) * mask


def gather_heads(full, mask, heads):
    total = None
    for h in range(heads):
        rows = slice(h * PAD, (h + 1) * PAD)
        part = full[rows, :] * mask[rows, :].astype(F32)
        total = part if total is None else total + part
    return total


def pair_index(rel_ref):
    lane = lax.broadcasted_iota(jnp.int32, (POSITIONS, 2 * PAD), 1)
    sub = lax.broadcasted_iota(jnp.int32, (POSITIONS, 2 * PAD), 0)
    same = (lax.rem(lane, PAD) == sub).astype(BF16)
    spread = dot((rel_ref[...] + 1).astype(F32).astype(BF16), same, TN)
    zero = jnp.zeros((PAD - POSITIONS, 2 * PAD), F32)
    return jnp.concatenate([spread, zero], axis=0).astype(jnp.int32)


def attn_forward_kernel(
    x_ref, gain_ref, shift_ref, wqkv_ref, qvb_ref, table_ref, rel_ref, reg_ref, order_ref,
    group_ref, perm_ref, hmask_ref, wproj_ref,
    part_ref, n1_ref, qkvw_ref, prob_ref, otok_ref,
    bm_ref, ow_ref, tab_ref,
):
    inner = wproj_ref.shape[0]
    heads = inner // HEAD_DIM
    lanes = heads * PAD
    unit, _ = normed(x_ref[...].astype(F32))
    n1 = (unit * gain_ref[...] + shift_ref[...]).astype(BF16)
    n1_ref[...] = n1
    q = ((dot(n1, wqkv_ref[0]) + qvb_ref[0:1, :]) * (HEAD_DIM ** (-0.5))).astype(BF16)
    k = dot(n1, wqkv_ref[1]).astype(BF16)
    v = (dot(n1, wqkv_ref[2]) + qvb_ref[1:2, :]).astype(BF16)
    perm = perm_ref[...]
    qkvw_ref[:, :inner] = dot(perm, q).astype(BF16)
    qkvw_ref[:, inner : 2 * inner] = dot(perm, k).astype(BF16)
    qkvw_ref[:, 2 * inner :] = dot(perm, v).astype(BF16)

    rel = pair_index(rel_ref)
    width = rel.shape[1]
    pairs = lanes // width
    tab_ref[...] = dot(table_ref[...], group_ref[...], TN, lax.Precision.HIGHEST)

    def pick(t, acc):
        hit = rel == t + 1
        row = tab_ref[pl.ds(t, 1), :]
        return tuple(
            jnp.where(hit, row[:, p * width : (p + 1) * width], acc[p]) for p in range(pairs)
        )

    zero = jnp.zeros(rel.shape, F32)
    picked = lax.fori_loop(0, tab_ref.shape[0], pick, (zero,) * pairs)
    bias = jnp.concatenate(picked, axis=1)
    region = jnp.broadcast_to((reg_ref[...] + 1).astype(F32), (16, reg_ref.shape[1])).astype(BF16)
    order = order_ref[...]
    across = dot(region, order, NT)
    down = dot(order, region, NT)
    for w in range(WINDOWS):
        rows = slice(w * PAD, (w + 1) * PAD)
        hit = down[rows, 0:1] == jnp.concatenate([across[0:1, rows]] * heads, axis=1)
        bm_ref[rows, :] = jnp.where(hit, bias, MASKED)

    def window(i, carry):
        rows = pl.ds(pl.multiple_of(i * PAD, PAD), PAD)
        hmask = hmask_ref[...]
        qw = qkvw_ref[rows, :inner]
        kw = qkvw_ref[rows, inner : 2 * inner]
        vw = qkvw_ref[rows, 2 * inner :]
        brows = pl.ds(pl.multiple_of(lax.rem(i, WINDOWS) * PAD, PAD), PAD)
        s = dot(kw, spread_heads(qw, hmask), NT) + bm_ref[brows, :]
        e = jnp.exp(s - jnp.max(s, axis=0, keepdims=True))
        p = e * (1.0 / jnp.sum(e, axis=0, keepdims=True))
        prob_ref[rows, :] = p
        full = dot(p.astype(BF16), vw, TN)
        ow_ref[rows, :] = gather_heads(full, hmask, heads).astype(BF16)
        return carry

    lax.fori_loop(0, qkvw_ref.shape[0] // PAD, window, 0)
    otok = dot(perm, ow_ref[...], TN).astype(BF16)
    otok_ref[...] = otok
    part_ref[...] = dot(otok, wproj_ref[...]).astype(BF16)


def mlp_kernel(
    x_ref, own_ref, recv_ref, pbias_ref, gain_ref, shift_ref, w1_ref, b1_ref, w2_ref, dy_ref,
    back_ref, h1_ref, n2_ref, act_ref, dub_ref, gb1_ref, gb2_ref,
    acc_ref,
):
    step = pl.program_id(0)

    @pl.when(step == 0)
    def _():
        h1 = (
            x_ref[...].astype(F32)
            + (own_ref[...].astype(F32) + recv_ref[...].astype(F32))
            + pbias_ref[...]
        )
        h1_ref[...] = h1
        unit, _ = normed(h1)
        n2_ref[...] = (unit * gain_ref[...] + shift_ref[...]).astype(BF16)
        gb2_ref[...] = jnp.sum(dy_ref[...].astype(F32), axis=0, keepdims=True)
        acc_ref[...] = jnp.zeros_like(acc_ref)

    u = dot(n2_ref[...], w1_ref[...]) + b1_ref[...]
    cdf = 0.5 * (1.0 + lax.erf(u * 0.7071067811865476))
    act_ref[...] = (u * cdf).astype(BF16)
    slope = cdf + u * jnp.exp(-0.5 * u * u) * 0.3989422804014327
    du = dot(dy_ref[...], w2_ref[...], NT) * slope
    gb1_ref[...] = jnp.sum(du, axis=0, keepdims=True)
    dub = du.astype(BF16)
    dub_ref[...] = dub
    acc_ref[...] += dot(dub, w1_ref[...], NT)

    @pl.when(step == pl.num_programs(0) - 1)
    def _():
        back_ref[...] = acc_ref[...].astype(BF16)


def half(ref, which, size):
    return ref[:, pl.ds(pl.multiple_of(which * size, size), size)]


def mlp_grad_kernel(bit_ref, act_ref, dub_ref, n2_ref, dy_ref, w2_ref, keep_ref, send_ref, part_ref):
    bit = bit_ref[0]
    size = act_ref.shape[1] // 2
    for out, which in ((send_ref, 1 - bit), (keep_ref, bit)):
        out[:size, :] = dot(half(act_ref, which, size), dy_ref[...], TN).astype(BF16)
        out[size:, :] = dot(n2_ref[...], half(dub_ref, which, size), TN).astype(BF16)
    part_ref[...] = dot(act_ref[...], w2_ref[...]).astype(BF16)


def attn_backward_kernel(
    dy_ref, own_ref, recv_ref, h1_ref, gain_ref, wproj_ref, qkvw_ref, prob_ref, perm_ref,
    hmask_ref, wqkv_ref,
    part_ref, dh_ref, dhb_ref, dp_ref, sums_ref, dsum_ref,
    dow_ref, dqkv_ref,
):
    inner = wproj_ref.shape[0]
    heads = inner // HEAD_DIM
    dn2 = own_ref[...].astype(F32) + recv_ref[...].astype(F32)
    unit, inverse = normed(h1_ref[...])
    sums_ref[0:1, :] = jnp.sum(dn2 * unit, axis=0, keepdims=True)
    sums_ref[1:2, :] = jnp.sum(dn2, axis=0, keepdims=True)
    dh = dy_ref[...].astype(F32) + norm_backward(dn2, unit, inverse, gain_ref[...])
    dh_ref[...] = dh
    sums_ref[2:3, :] = jnp.sum(dh, axis=0, keepdims=True)
    dhb = dh.astype(BF16)
    dhb_ref[...] = dhb
    perm = perm_ref[...]
    dow_ref[...] = dot(perm, dot(dhb, wproj_ref[...], NT).astype(BF16)).astype(BF16)
    dsum_ref[...] = jnp.zeros_like(dsum_ref)

    def window(i, carry):
        qsum, vsum = carry
        rows = pl.ds(pl.multiple_of(i * PAD, PAD), PAD)
        hmask = hmask_ref[...]
        qblk = spread_heads(qkvw_ref[rows, :inner], hmask)
        kw = qkvw_ref[rows, inner : 2 * inner]
        vw = qkvw_ref[rows, 2 * inner :]
        oblk = spread_heads(dow_ref[rows, :], hmask)
        p = prob_ref[rows, :]
        dp = dot(vw, oblk, NT)
        ds = p * (dp - jnp.sum(p * dp, axis=0, keepdims=True))
        dsum_ref[...] += ds
        dsb = ds.astype(BF16)
        dq = gather_heads(dot(dsb, kw, TN), hmask, heads) * (HEAD_DIM ** (-0.5))
        dk = dot(dsb, qblk)
        dv = dot(p.astype(BF16), oblk)
        dqkv_ref[rows, :inner] = dq.astype(BF16)
        dqkv_ref[rows, inner : 2 * inner] = dk.astype(BF16)
        dqkv_ref[rows, 2 * inner :] = dv.astype(BF16)
        return (
            qsum + jnp.sum(dq, axis=0, keepdims=True),
            vsum + jnp.sum(dv, axis=0, keepdims=True),
        )

    zero = jnp.zeros((1, inner), F32)
    qsum, vsum = lax.fori_loop(0, qkvw_ref.shape[0] // PAD, window, (zero, zero))
    sums_ref[3:4, :inner] = qsum
    sums_ref[3:4, inner:] = vsum
    dp_tok = dot(perm, dqkv_ref[...], TN).astype(BF16)
    dp_ref[...] = dp_tok
    part = dot(dp_tok[:, :inner], wqkv_ref[0], NT)
    part = part + dot(dp_tok[:, inner : 2 * inner], wqkv_ref[1], NT)
    part_ref[...] = (part + dot(dp_tok[:, 2 * inner :], wqkv_ref[2], NT)).astype(BF16)


def attn_grad_kernel(bit_ref, n1_ref, dp_ref, otok_ref, dhb_ref, keep_ref, send_ref):
    bit = bit_ref[0]
    wide = dp_ref.shape[1]
    rows = n1_ref.shape[1] // 2
    for out, which in ((send_ref, 1 - bit), (keep_ref, bit)):
        out[:, :wide] = dot(half(n1_ref, which, rows), dp_ref[...], TN).astype(BF16)
        out[:, wide:] = dot(otok_ref[...], half(dhb_ref, which, rows), TN).astype(BF16)


def table_kernel(dsum_ref, rel_ref, group_ref, out_ref, tab_ref):
    rel = pair_index(rel_ref)
    width = rel.shape[1]
    pairs = dsum_ref.shape[1] // width

    def eight(n, carry):
        for p in range(pairs):
            cols = slice(p * width, (p + 1) * width)
            part = dsum_ref[:, cols]
            found = [
                jnp.sum(jnp.where(rel == n * 8 + t + 1, part, 0.0), axis=0, keepdims=True)
                for t in range(8)
            ]
            tab_ref[pl.ds(pl.multiple_of(n * 8, 8), 8), cols] = jnp.concatenate(found, axis=0)
        return carry

    lax.fori_loop(0, tab_ref.shape[0] // 8, eight, 0)
    out_ref[...] = dot(group_ref[...], tab_ref[...], NT, lax.Precision.HIGHEST)


def input_grad_kernel(
    x_ref, own_ref, recv_ref, dh_ref, gain_ref, sums_ref, gb1_ref, gb2_ref, tab_ref,
    gin_ref, small_ref,
):
    width = x_ref.shape[1]
    unit, inverse = normed(x_ref[...].astype(F32))
    dn1 = own_ref[...].astype(F32) + recv_ref[...].astype(F32)
    gin_ref[...] = dh_ref[...] + norm_backward(dn1, unit, inverse, gain_ref[...])
    small_ref[...] = jnp.zeros_like(small_ref)
    small_ref[0:1, :] = jnp.sum(dn1 * unit, axis=0, keepdims=True)
    small_ref[1:2, :] = jnp.sum(dn1, axis=0, keepdims=True)
    small_ref[2:6, :] = sums_ref[...]
    small_ref[6:7, :] = gb2_ref[...]
    at = 7
    for n in range(gb1_ref.shape[1] // width):
        small_ref[at : at + 1, :] = gb1_ref[:, n * width : (n + 1) * width]
        at += 1
    for h in range(tab_ref.shape[0]):
        small_ref[at : at + 1, : tab_ref.shape[1]] = tab_ref[h : h + 1, :]
        at += 1


def small_kernel(
    left_ref, right_ref,
    gain1_ref, shift1_ref, gain2_ref, shift2_ref, pbias_ref, qvb_ref, gb2_ref, gb1_ref, tab_ref,
):
    small = left_ref[...] + right_ref[...]
    width = small.shape[1]
    inner = qvb_ref.shape[1]
    for n, out in enumerate((gain1_ref, shift1_ref, gain2_ref, shift2_ref, pbias_ref)):
        out[...] = small[n : n + 1, :]
    qvb_ref[0:1, :] = small[5:6, :inner]
    qvb_ref[1:2, :] = small[5:6, inner:]
    gb2_ref[...] = small[6:7, :]
    at = 7
    for n in range(gb1_ref.shape[1] // width):
        gb1_ref[:, n * width : (n + 1) * width] = small[at : at + 1, :]
        at += 1
    tab_ref[...] = small[at : at + tab_ref.shape[0], : tab_ref.shape[1]]


def mlp_finish_kernel(bit_ref, mine_ref, other_ref, fc2_ref, fc1_ref):
    half_rows = fc2_ref.shape[0] // 2
    for src, which in ((mine_ref, bit_ref[0]), (other_ref, 1 - bit_ref[0])):
        at = pl.ds(pl.multiple_of(which * half_rows, half_rows), half_rows)
        fc2_ref[at, :] = src[:half_rows, :].astype(F32)
        fc1_ref[:, at] = src[half_rows:, :].astype(F32)


def attn_finish_kernel(bit_ref, mine_ref, other_ref, qkv_ref, proj_ref):
    inner = qkv_ref.shape[2]
    half_rows = qkv_ref.shape[1] // 2
    block = half_rows // 4
    for src, which in ((mine_ref, bit_ref[0]), (other_ref, 1 - bit_ref[0])):
        for n in range(3):
            for a in range(2):
                for b in range(2):
                    to = pl.multiple_of(which * half_rows + (b * 2 + a) * block, block)
                    rows = slice((a * 2 + b) * block, (a * 2 + b + 1) * block)
                    cols = slice(n * inner, (n + 1) * inner)
                    qkv_ref[n, pl.ds(to, block), :] = src[rows, cols].astype(F32)
        at = pl.ds(pl.multiple_of(which * half_rows, half_rows), half_rows)
        for a in range(2):
            for b in range(2):
                rows = slice((a * 2 + b) * block, (a * 2 + b + 1) * block)
                to = slice((b * 2 + a) * block, (b * 2 + a + 1) * block)
                proj_ref[to, at] = src[rows, 3 * inner :].astype(F32)


def output_kernel(h1_ref, own_ref, recv_ref, bias_ref, out_ref):
    total = own_ref[...].astype(F32) + recv_ref[...].astype(F32)
    out_ref[...] = (h1_ref[...] + total + bias_ref[...]).astype(BF16)


def shape(dims, dtype):
    return jax.ShapeDtypeStruct(dims, dtype)


VMEM = functools.partial(pl.BlockSpec, memory_space=pltpu.VMEM)
SMEM = functools.partial(pl.BlockSpec, memory_space=pltpu.SMEM)


def swap(value, axis, size, bit):
    return lax.ppermute(value, axis, [(i, i ^ bit) for i in range(size)])


def add_pair(left, right):
    return left.astype(F32) + right.astype(F32)


def reduce_scatter(keep, send, bits, size):
    index = lax.axis_index("dp")
    for n, bit in enumerate(bits):
        recv = swap(send, "dp", size, bit)
        keep = add_pair(keep, recv).astype(BF16)
        if n + 1 < len(bits):
            rows = keep.shape[0] // 2
            low, high = keep[:rows], keep[rows:]
            upper = (index & bits[n + 1]) != 0
            keep, send = jnp.where(upper, high, low), jnp.where(upper, low, high)
    return keep


def gather_back(value, bits, size):
    index = lax.axis_index("dp")
    for bit in bits[:-1]:
        other = swap(value, "dp", size, bit)
        upper = (index & bit) != 0
        value = jnp.concatenate(
            [jnp.where(upper, other, value), jnp.where(upper, value, other)], axis=0
        )
    return value, swap(value, "dp", size, bits[-1])


def local(
    dp_size,
    inputs,
    ln1_gain,
    ln1_shift,
    w_qkv,
    qv_bias,
    bias_table,
    rel_index,
    regions,
    w_proj,
    proj_bias,
    ln2_gain,
    ln2_shift,
    w_fc1,
    fc1_bias,
    w_fc2,
    fc2_bias,
    grad_output,
):
    tokens, width = inputs.shape
    images = tokens // (SIDE * SIDE)
    inner = w_qkv.shape[2]
    heads = inner // HEAD_DIM
    lanes = heads * PAD
    wrows = images * WINDOWS * PAD
    hidden = w_fc1.shape[1]
    table_rows = bias_table.shape[0]
    table_pad = -(-table_rows // 8) * 8
    row = lambda v: v.reshape(1, -1)

    def tensor_swap(value):
        return swap(value, "tensor", 2, 1)

    bits = [1 << n for n in range(dp_size.bit_length() - 1)]
    core_bit = (lax.axis_index("dp") & 1).astype(jnp.int32).reshape(1)

    order = window_order()
    perm = jnp.asarray(np.kron(np.eye(images, dtype=np.float32), order), BF16)
    shifted = jnp.asarray(window_order(0), BF16)
    hmask = jnp.asarray(
        np.kron(np.eye(heads, dtype=np.float32), np.ones((PAD, HEAD_DIM), np.float32)), BF16
    )
    group = jnp.asarray(np.kron(np.eye(heads, dtype=np.float32), np.ones((1, PAD), np.float32)))
    qkv_weight = w_qkv.transpose(1, 0, 2)

    attn_part, n1, qkvw, prob, otok = pl.pallas_call(
        attn_forward_kernel,
        out_shape=(
            shape((tokens, width), BF16),
            shape((tokens, width), BF16),
            shape((wrows, 3 * inner), BF16),
            shape((wrows, lanes), F32),
            shape((tokens, inner), BF16),
        ),
        scratch_shapes=[
            pltpu.VMEM((WINDOWS * PAD, lanes), F32),
            pltpu.VMEM((wrows, inner), BF16),
            pltpu.VMEM((table_rows, lanes), F32),
        ],
        name="attn_forward",
    )(
        inputs, row(ln1_gain), row(ln1_shift), qkv_weight, qv_bias, bias_table.T, rel_index,
        row(regions), shifted, group, perm, hmask, w_proj,
    )
    attn_recv = tensor_swap(attn_part)

    steps = hidden // HIDDEN_BLOCK
    full = lambda dims: pl.BlockSpec(dims, lambda j: (0, 0))
    cols = lambda rows: pl.BlockSpec((rows, HIDDEN_BLOCK), lambda j: (0, j))
    back_two_part, h1, n2, act, dub, grad_b1, grad_b2 = pl.pallas_call(
        mlp_kernel,
        grid=(steps,),
        in_specs=[
            full((tokens, width)), full((tokens, width)), full((tokens, width)), full((1, width)),
            full((1, width)), full((1, width)), cols(width), cols(1),
            pl.BlockSpec((HIDDEN_BLOCK, width), lambda j: (j, 0)), full((tokens, width)),
        ],
        out_specs=(
            full((tokens, width)), full((tokens, width)), full((tokens, width)), cols(tokens),
            cols(tokens), cols(1), full((1, width)),
        ),
        out_shape=(
            shape((tokens, width), BF16),
            shape((tokens, width), F32),
            shape((tokens, width), BF16),
            shape((tokens, hidden), BF16),
            shape((tokens, hidden), BF16),
            shape((1, hidden), F32),
            shape((1, width), F32),
        ),
        scratch_shapes=[pltpu.VMEM((tokens, width), F32)],
        name="mlp",
    )(
        inputs, attn_part, attn_recv, row(proj_bias), row(ln2_gain), row(ln2_shift), w_fc1,
        row(fc1_bias), w_fc2, grad_output,
    )
    back_two_recv = tensor_swap(back_two_part)

    keep, send, mlp_part = pl.pallas_call(
        mlp_grad_kernel,
        in_specs=[SMEM()] + [VMEM()] * 5,
        out_shape=(
            shape((hidden // 2 + width, width), BF16),
            shape((hidden // 2 + width, width), BF16),
            shape((tokens, width), BF16),
        ),
        cost_estimate=pl.CostEstimate(
            flops=6 * tokens * hidden * width, bytes_accessed=8 << 20, transcendentals=0
        ),
        name="mlp_grad",
    )(core_bit, act, dub, n2, grad_output, w_fc2)
    mlp_shard = reduce_scatter(keep, send, bits, dp_size)

    back_one_part, dh, dhb, dproj, sums, dsum = pl.pallas_call(
        attn_backward_kernel,
        out_shape=(
            shape((tokens, width), BF16),
            shape((tokens, width), F32),
            shape((tokens, width), BF16),
            shape((tokens, 3 * inner), BF16),
            shape((4, width), F32),
            shape((PAD, lanes), F32),
        ),
        scratch_shapes=[
            pltpu.VMEM((wrows, inner), BF16),
            pltpu.VMEM((wrows, 3 * inner), BF16),
        ],
        name="attn_backward",
    )(
        grad_output, back_two_part, back_two_recv, h1, row(ln2_gain), w_proj, qkvw, prob, perm,
        hmask, qkv_weight,
    )
    back_one_recv = tensor_swap(back_one_part)

    keep, send = pl.pallas_call(
        attn_grad_kernel,
        in_specs=[SMEM()] + [VMEM()] * 4,
        out_shape=(
            shape((width // 2, 3 * inner + inner), BF16),
            shape((width // 2, 3 * inner + inner), BF16),
        ),
        cost_estimate=pl.CostEstimate(
            flops=8 * tokens * inner * width, bytes_accessed=4 << 20, transcendentals=0
        ),
        name="attn_grad",
    )(core_bit, n1, dproj, otok, dhb)
    attn_shard = reduce_scatter(keep, send, bits, dp_size)

    table_sum = pl.pallas_call(
        table_kernel,
        out_shape=shape((heads, table_pad), F32),
        scratch_shapes=[pltpu.VMEM((table_pad, lanes), F32)],
        name="table",
    )(dsum, rel_index, group)

    mlp_recv = tensor_swap(mlp_part)
    output = pl.pallas_call(
        output_kernel, out_shape=shape((tokens, width), BF16), name="output"
    )(h1, mlp_part, mlp_recv, row(fc2_bias))

    small_rows = 7 + hidden // width + heads
    grad_input, small = pl.pallas_call(
        input_grad_kernel,
        out_shape=(shape((tokens, width), F32), shape((small_rows, width), F32)),
        name="input_grad",
    )(
        inputs, back_one_part, back_one_recv, dh, row(ln1_gain), sums, grad_b1, grad_b2, table_sum
    )
    for n, bit in enumerate(reversed(bits)):
        recv = swap(small, "dp", dp_size, bit)
        if n + 1 < len(bits):
            small = small + recv
    smalls = pl.pallas_call(
        small_kernel,
        out_shape=tuple(shape((1, width), F32) for _ in range(5))
        + (
            shape((2, inner), F32),
            shape((1, width), F32),
            shape((1, hidden), F32),
            shape((heads, table_rows), F32),
        ),
        name="small",
    )(small, recv)
    grad_gain1, grad_shift1, grad_gain2, grad_shift2, grad_pb, grad_qvb, grad_b2, grad_b1 = smalls[:8]

    down = bits[::-1]
    mine, other = gather_back(mlp_shard, down, dp_size)
    grad_fc2, grad_fc1 = pl.pallas_call(
        mlp_finish_kernel,
        in_specs=[SMEM()] + [VMEM()] * 2,
        out_shape=(shape((hidden, width), F32), shape((width, hidden), F32)),
        name="mlp_finish",
    )(core_bit, mine, other)
    mine, other = gather_back(attn_shard, down[:-3] + [down[-2], down[-3], down[-1]], dp_size)
    grad_qkv, grad_proj = pl.pallas_call(
        attn_finish_kernel,
        in_specs=[SMEM()] + [VMEM()] * 2,
        out_shape=(shape((3, width, inner), F32), shape((inner, width), F32)),
        name="attn_finish",
    )(core_bit, mine, other)

    flat = lambda v: v.reshape(-1)
    return (
        output, grad_input, flat(grad_gain1), flat(grad_shift1), grad_qkv.transpose(1, 0, 2),
        grad_qvb, smalls[8].T, grad_proj, flat(grad_pb), flat(grad_gain2), flat(grad_shift2),
        grad_fc1, flat(grad_b1), grad_fc2, flat(grad_b2),
    )


def solution(mesh):
    size = mesh.shape["dp"]

    def body(*args):
        return local(size, *args)

    return jax.shard_map(
        body,
        mesh=mesh,
        in_specs=(
            P("dp", None),
            P(),
            P(),
            P(None, None, "tensor"),
            P(None, "tensor"),
            P(None, "tensor"),
            P(),
            P(),
            P("tensor", None),
            P(),
            P(),
            P(),
            P(None, "tensor"),
            P("tensor"),
            P("tensor", None),
            P(),
            P("dp", None),
        ),
        out_specs=(
            P("dp", None),
            P("dp", None),
            P(),
            P(),
            P(None, None, "tensor"),
            P(None, "tensor"),
            P(None, "tensor"),
            P("tensor", None),
            P(),
            P(),
            P(),
            P(None, "tensor"),
            P("tensor"),
            P("tensor", None),
            P(),
        ),
        check_vma=False,
    )
```

```python
import functools

import numpy as np
import jax
import jax.numpy as jnp
from jax import lax
from jax.experimental import pallas as pl
from jax.experimental.pallas import tpu as pltpu
from jax.sharding import PartitionSpec as P

HEAD_DIM = 32
SIDE = 14
WIN = 7
SHIFT = 3
ACROSS = SIDE // WIN
POSITIONS = WIN * WIN
PAD = 64
WINDOWS = ACROSS * ACROSS

NORM_EPS = 1e-05
MASKED = -1e30
F32 = jnp.float32
BF16 = jnp.bfloat16
HIDDEN_BLOCK = 256


def dot(a, b, dims=((1,), (0,)), precision=None):
    return lax.dot_general(a, b, (dims, ((), ())), preferred_element_type=F32, precision=precision)


NT = ((1,), (1,))
TN = ((0,), (0,))


def normed(values):
    centered = values - jnp.mean(values, axis=-1, keepdims=True)
    inverse = lax.rsqrt(jnp.mean(centered * centered, axis=-1, keepdims=True) + NORM_EPS)
    return centered * inverse, inverse


def norm_backward(upstream, unit, inverse, gain):
    weighted = upstream * gain
    return inverse * (
        weighted
        - jnp.mean(weighted, axis=-1, keepdims=True)
        - unit * jnp.mean(weighted * unit, axis=-1, keepdims=True)
    )


def window_order(shift=SHIFT):
    order = np.zeros((WINDOWS * PAD, SIDE * SIDE), np.float32)
    for a in range(ACROSS):
        for b in range(ACROSS):
            for i in range(POSITIONS):
                row = (a * WIN + i // WIN + shift) % SIDE
                col = (b * WIN + i % WIN + shift) % SIDE
                order[(a * ACROSS + b) * PAD + i, row * SIDE + col] = 1.0
    return order


GROUP = 128 // HEAD_DIM


def head_lanes(dtype):
    lane = lax.broadcasted_iota(jnp.int32, (PAD, 128), 1) // HEAD_DIM
    return [(lane == h).astype(dtype) for h in range(GROUP)]


def spread_heads(tile, masks):
    return jnp.concatenate([tile * mask for mask in masks], axis=0)


def gather_heads(full):
    lane = lax.broadcasted_iota(jnp.int32, (PAD, 128), 1) // HEAD_DIM
    total = full[:PAD, :]
    for h in range(1, GROUP):
        total = jnp.where(lane == h, full[h * PAD : (h + 1) * PAD, :], total)
    return total


def slab(image):
    start = image * SIDE * SIDE // 8 * 8
    return start, -(-SIDE * SIDE // 8) * 8, image * SIDE * SIDE - start


def own_rows(image, rows):
    offset = slab(image)[2]
    at = lax.broadcasted_iota(jnp.int32, (rows, 1), 0)
    return ((at >= offset) & (at < offset + SIDE * SIDE)).astype(F32)


def pair_index(rel_ref):
    lane = lax.broadcasted_iota(jnp.int32, (POSITIONS, 2 * PAD), 1)
    sub = lax.broadcasted_iota(jnp.int32, (POSITIONS, 2 * PAD), 0)
    same = (lax.rem(lane, PAD) == sub).astype(BF16)
    spread = dot((rel_ref[...] + 1).astype(F32).astype(BF16), same, TN)
    zero = jnp.zeros((PAD - POSITIONS, 2 * PAD), F32)
    return jnp.concatenate([spread, zero], axis=0).astype(jnp.int32)


def bias_kernel(table_ref, rel_ref, reg_ref, order_ref, bm_ref):
    heads, entries = table_ref.shape
    index = pair_index(rel_ref) - 1
    first = jnp.clip(index, 0, 127)
    second = jnp.clip(index - 128, 0, 127)
    left = lax.broadcasted_iota(jnp.int32, index.shape, 1) < PAD

    def pick(h):
        low = jnp.broadcast_to(table_ref[h : h + 1, :128], index.shape)
        high = jnp.concatenate(
            [table_ref[h : h + 1, 128:], jnp.zeros((1, 256 - entries), F32)], axis=1
        )
        high = jnp.broadcast_to(high, index.shape)
        return jnp.where(
            index < 128,
            jnp.take_along_axis(low, first, axis=1),
            jnp.take_along_axis(high, second, axis=1),
        )

    region = jnp.broadcast_to((reg_ref[...] + 1).astype(F32), (16, reg_ref.shape[1])).astype(BF16)
    order = order_ref[...]
    across = dot(region, order, NT)
    down = dot(order, region, NT)
    hits = []
    for w in range(WINDOWS):
        rows = slice(w * PAD, (w + 1) * PAD)
        hits.append(down[rows, 0:1] == jnp.concatenate([across[0:1, rows]] * 2, axis=1))
    for p in range(heads // 2):
        bias = jnp.where(left, pick(2 * p), pick(2 * p + 1))
        for w in range(WINDOWS):
            rows = slice(w * PAD, (w + 1) * PAD)
            bm_ref[rows, p * 128 : (p + 1) * 128] = jnp.where(hits[w], bias, MASKED)


def attn_forward_kernel(
    image, x_ref, gain_ref, shift_ref, wqkv_ref, qvb_ref, bm_ref, perm_ref, wproj_ref,
    part_ref, n1_ref, qkvw_ref, prob_ref, otok_ref,
    ow_ref,
):
    inner = wproj_ref.shape[0]
    start, size, _ = slab(image)
    unit, _ = normed(x_ref[start : start + size, :].astype(F32))
    n1 = (unit * gain_ref[...] + shift_ref[...]).astype(BF16)
    n1_ref[...] = n1
    q = ((dot(n1, wqkv_ref[0]) + qvb_ref[0:1, :]) * (HEAD_DIM ** (-0.5))).astype(BF16)
    k = dot(n1, wqkv_ref[1]).astype(BF16)
    v = (dot(n1, wqkv_ref[2]) + qvb_ref[1:2, :]).astype(BF16)
    perm = perm_ref[...]
    qkvw_ref[:, :inner] = dot(perm, q).astype(BF16)
    qkvw_ref[:, inner : 2 * inner] = dot(perm, k).astype(BF16)
    qkvw_ref[:, 2 * inner :] = dot(perm, v).astype(BF16)

    def window(i, carry):
        rows = pl.ds(pl.multiple_of(i * PAD, PAD), PAD)
        masks = head_lanes(BF16)
        for g in range(inner // 128):
            cols = slice(g * 128, (g + 1) * 128)
            wide = slice(g * GROUP * PAD, (g + 1) * GROUP * PAD)
            at = lambda n: slice(n * inner + g * 128, n * inner + (g + 1) * 128)
            spread = spread_heads(qkvw_ref[rows, at(0)], masks)
            s = dot(qkvw_ref[rows, at(1)], spread, NT) + bm_ref[rows, wide]
            e = jnp.exp(s - jnp.max(s, axis=0, keepdims=True))
            p = e * (1.0 / jnp.sum(e, axis=0, keepdims=True))
            prob_ref[rows, wide] = p
            full = dot(p.astype(BF16), qkvw_ref[rows, at(2)], TN)
            ow_ref[rows, cols] = gather_heads(full).astype(BF16)
        return carry

    lax.fori_loop(0, WINDOWS, window, 0)
    otok = dot(perm, ow_ref[...], TN).astype(BF16)
    otok_ref[...] = otok
    part_ref[...] = dot(otok, wproj_ref[...]).astype(BF16)


def mlp_kernel(
    x_ref, own0_ref, recv0_ref, own1_ref, recv1_ref, pbias_ref, gain_ref, shift_ref, w1_ref,
    b1_ref, w2_ref, dy_ref,
    back_ref, h1_ref, n2_ref, act_ref, dub_ref, gb1_ref, gb2_ref,
    acc_ref,
):
    step = pl.program_id(0)

    @pl.when(step == 0)
    def _():
        h1_ref[...] = x_ref[...].astype(F32) + pbias_ref[...]
        for image, (own, recv) in enumerate(((own0_ref, recv0_ref), (own1_ref, recv1_ref))):
            start, size, _ = slab(image)
            total = own[...].astype(F32) + recv[...].astype(F32)
            h1_ref[start : start + size, :] += total
        unit, _ = normed(h1_ref[...])
        n2_ref[...] = (unit * gain_ref[...] + shift_ref[...]).astype(BF16)
        gb2_ref[...] = jnp.sum(dy_ref[...].astype(F32), axis=0, keepdims=True)
        acc_ref[...] = jnp.zeros_like(acc_ref)

    u = dot(n2_ref[...], w1_ref[...]) + b1_ref[...]
    cdf = 0.5 * (1.0 + lax.erf(u * 0.7071067811865476))
    act_ref[...] = (u * cdf).astype(BF16)
    slope = cdf + u * jnp.exp(-0.5 * u * u) * 0.3989422804014327
    du = dot(dy_ref[...], w2_ref[...], NT) * slope
    gb1_ref[...] = jnp.sum(du, axis=0, keepdims=True)
    dub = du.astype(BF16)
    dub_ref[...] = dub
    acc_ref[...] += dot(dub, w1_ref[...], NT)

    @pl.when(step == pl.num_programs(0) - 1)
    def _():
        back_ref[...] = acc_ref[...].astype(BF16)


def half(ref, which, size):
    return ref[:, pl.ds(pl.multiple_of(which * size, size), size)]


def mlp_grad_kernel(flip, bit_ref, act_ref, dub_ref, n2_ref, dy_ref, out_ref):
    which = bit_ref[0] if flip == 0 else 1 - bit_ref[0]
    size = act_ref.shape[1] // 2
    width = dy_ref.shape[1]
    out_ref[:, :width] = dot(half(act_ref, which, size), dy_ref[...], TN).astype(BF16)
    out_ref[:, width:] = dot(n2_ref[...], half(dub_ref, which, size), TN).astype(BF16)


def mlp_out_kernel(act_ref, w2_ref, part_ref):
    part_ref[...] = dot(act_ref[...], w2_ref[...]).astype(BF16)


def attn_backward_kernel(
    image, dy_ref, own_ref, recv_ref, h1_ref, gain_ref, wproj_ref, qkvw_ref, prob_ref, perm_ref,
    wqkv_ref,
    part_ref, dh_ref, dhb_ref, dp_ref, sums_ref, dsum_ref,
    dow_ref, dqkv_ref,
):
    inner = wproj_ref.shape[0]
    start, size, _ = slab(image)
    slab_rows = slice(start, start + size)
    mask = own_rows(image, size)
    dn2 = own_ref[slab_rows, :].astype(F32) + recv_ref[slab_rows, :].astype(F32)
    unit, inverse = normed(h1_ref[slab_rows, :])
    mine = dn2 * mask
    sums_ref[0:1, :] = jnp.sum(mine * unit, axis=0, keepdims=True)
    sums_ref[1:2, :] = jnp.sum(mine, axis=0, keepdims=True)
    dh = dy_ref[slab_rows, :].astype(F32) + norm_backward(dn2, unit, inverse, gain_ref[...])
    dh_ref[...] = dh
    sums_ref[2:3, :] = jnp.sum(dh * mask, axis=0, keepdims=True)
    dhb = dh.astype(BF16)
    dhb_ref[...] = dhb
    perm = perm_ref[...]
    dow_ref[...] = dot(perm, dot(dhb, wproj_ref[...], NT).astype(BF16)).astype(BF16)
    dsum_ref[...] = jnp.zeros_like(dsum_ref)
    groups = inner // 128

    def window(i, carry):
        rows = pl.ds(pl.multiple_of(i * PAD, PAD), PAD)
        masks = head_lanes(BF16)
        sums = []
        for g in range(groups):
            wide = slice(g * GROUP * PAD, (g + 1) * GROUP * PAD)
            at = lambda n: slice(n * inner + g * 128, n * inner + (g + 1) * 128)
            qblk = spread_heads(qkvw_ref[rows, at(0)], masks)
            oblk = spread_heads(dow_ref[rows, at(0)], masks)
            p = prob_ref[rows, wide]
            dp = dot(qkvw_ref[rows, at(2)], oblk, NT)
            ds = p * (dp - jnp.sum(p * dp, axis=0, keepdims=True))
            dsum_ref[:, wide] += ds
            dsb = ds.astype(BF16)
            dq = gather_heads(dot(dsb, qkvw_ref[rows, at(1)], TN)) * (HEAD_DIM ** (-0.5))
            dv = dot(p.astype(BF16), oblk)
            dqkv_ref[rows, at(0)] = dq.astype(BF16)
            dqkv_ref[rows, at(1)] = dot(dsb, qblk).astype(BF16)
            dqkv_ref[rows, at(2)] = dv.astype(BF16)
            sums += [jnp.sum(dq, axis=0, keepdims=True), jnp.sum(dv, axis=0, keepdims=True)]
        return tuple(a + b for a, b in zip(carry, sums))

    zero = jnp.zeros((1, 128), F32)
    sums = lax.fori_loop(0, WINDOWS, window, (zero,) * (2 * groups))
    for g in range(groups):
        sums_ref[3:4, g * 128 : (g + 1) * 128] = sums[2 * g]
        sums_ref[3:4, inner + g * 128 : inner + (g + 1) * 128] = sums[2 * g + 1]
    dp_tok = dot(perm, dqkv_ref[...], TN).astype(BF16)
    dp_ref[...] = dp_tok
    part = dot(dp_tok[:, :inner], wqkv_ref[0], NT)
    part = part + dot(dp_tok[:, inner : 2 * inner], wqkv_ref[1], NT)
    part_ref[...] = (part + dot(dp_tok[:, 2 * inner :], wqkv_ref[2], NT)).astype(BF16)


def attn_grad_kernel(
    flip, bit_ref, n1a_ref, n1b_ref, dpa_ref, dpb_ref, oa_ref, ob_ref, dha_ref, dhb_ref, out_ref
):
    which = bit_ref[0] if flip == 0 else 1 - bit_ref[0]
    wide = dpa_ref.shape[1]
    rows = n1a_ref.shape[1] // 2
    qkv = dot(half(n1a_ref, which, rows), dpa_ref[...], TN)
    out_ref[:, :wide] = (qkv + dot(half(n1b_ref, which, rows), dpb_ref[...], TN)).astype(BF16)
    proj = dot(oa_ref[...], half(dha_ref, which, rows), TN)
    out_ref[:, wide:] = (proj + dot(ob_ref[...], half(dhb_ref, which, rows), TN)).astype(BF16)


def table_kernel(dsa_ref, dsb_ref, rel_ref, group_ref, out_ref, tab_ref, dsum_ref):
    rel = pair_index(rel_ref)
    width = rel.shape[1]
    pairs = dsum_ref.shape[1] // width
    dsum_ref[...] = dsa_ref[...] + dsb_ref[...]

    def eight(n, carry):
        for p in range(pairs):
            cols = slice(p * width, (p + 1) * width)
            part = dsum_ref[:, cols]
            found = [
                jnp.sum(jnp.where(rel == n * 8 + t + 1, part, 0.0), axis=0, keepdims=True)
                for t in range(8)
            ]
            tab_ref[pl.ds(pl.multiple_of(n * 8, 8), 8), cols] = jnp.concatenate(found, axis=0)
        return carry

    lax.fori_loop(0, tab_ref.shape[0] // 8, eight, 0)
    out_ref[...] = dot(group_ref[...], tab_ref[...], NT, lax.Precision.HIGHEST)


def input_grad_kernel(
    x_ref, own0_ref, recv0_ref, own1_ref, recv1_ref, dh0_ref, dh1_ref, gain_ref,
    sums0_ref, sums1_ref, gb1_ref, gb2_ref, tab_ref,
    gin_ref, small_ref,
):
    width = x_ref.shape[1]
    small_ref[...] = jnp.zeros_like(small_ref)
    for image, (own, recv, dh) in enumerate(
        ((own0_ref, recv0_ref, dh0_ref), (own1_ref, recv1_ref, dh1_ref))
    ):
        start, size, offset = slab(image)
        unit, inverse = normed(x_ref[start : start + size, :].astype(F32))
        dn1 = own[...].astype(F32) + recv[...].astype(F32)
        small_ref[0:1, :] += jnp.sum(dn1 * unit, axis=0, keepdims=True)
        small_ref[1:2, :] += jnp.sum(dn1, axis=0, keepdims=True)
        gin = dh[...] + norm_backward(dn1, unit, inverse, gain_ref[...])
        if offset == 0:
            gin_ref[start : start + size, :] = gin
        else:
            at = lax.broadcasted_iota(jnp.int32, (8, 1), 0)
            gin_ref[start : start + 8, :] = jnp.where(
                at < offset, gin_ref[start : start + 8, :], gin[:8, :]
            )
            gin_ref[start + 8 : start + size, :] = gin[8:, :]
    small_ref[2:6, :] = sums0_ref[...] + sums1_ref[...]
    small_ref[6:7, :] = gb2_ref[...]
    at = 7
    for n in range(gb1_ref.shape[1] // width):
        small_ref[at : at + 1, :] = gb1_ref[:, n * width : (n + 1) * width]
        at += 1
    for h in range(tab_ref.shape[0]):
        small_ref[at : at + 1, : tab_ref.shape[1]] = tab_ref[h : h + 1, :]
        at += 1


def small_kernel(
    left_ref, right_ref,
    gain1_ref, shift1_ref, gain2_ref, shift2_ref, pbias_ref, qvb_ref, gb2_ref, gb1_ref, tab_ref,
):
    small = left_ref[...] + right_ref[...]
    width = small.shape[1]
    inner = qvb_ref.shape[1]
    for n, out in enumerate((gain1_ref, shift1_ref, gain2_ref, shift2_ref, pbias_ref)):
        out[...] = small[n : n + 1, :]
    qvb_ref[0:1, :] = small[5:6, :inner]
    qvb_ref[1:2, :] = small[5:6, inner:]
    gb2_ref[...] = small[6:7, :]
    at = 7
    for n in range(gb1_ref.shape[1] // width):
        gb1_ref[:, n * width : (n + 1) * width] = small[at : at + 1, :]
        at += 1
    tab_ref[...] = small[at : at + tab_ref.shape[0], : tab_ref.shape[1]]


def mlp_finish_kernel(bits, index_ref, mine_ref, other_ref, fc2_ref, fc1_ref):
    index = index_ref[0]
    total, width = mine_ref.shape[0], fc2_ref.shape[1]
    rows = total >> len(bits)
    for n in range(1 << len(bits)):
        to = 0
        for place, bit in enumerate(bits):
            away = (n >> place) & 1
            set_here = lax.shift_right_logical(index, bit.bit_length() - 1) & 1
            to = to + ((1 - set_here) if away else set_here) * (rows << place)
        for src, away in ((mine_ref, 0), (other_ref, 1)):
            which = (index & 1) if away == 0 else 1 - (index & 1)
            block = src[n * rows : (n + 1) * rows, :]
            at = pl.multiple_of(which * total + to, 8)
            fc2_ref[pl.ds(at, rows), :] = block[:, :width].astype(F32)
            cols = pl.ds(pl.multiple_of(which * total, 128), total)
            fc1_ref[pl.ds(pl.multiple_of(to, 8), rows), cols] = block[:, width:].astype(F32)


def attn_finish_kernel(bit_ref, mine_ref, other_ref, qkv_ref, proj_ref):
    inner = qkv_ref.shape[2]
    half_rows = qkv_ref.shape[1] // 2
    block = half_rows // 4
    for src, which in ((mine_ref, bit_ref[0]), (other_ref, 1 - bit_ref[0])):
        for n in range(3):
            for a in range(2):
                for b in range(2):
                    to = pl.multiple_of(which * half_rows + (b * 2 + a) * block, block)
                    rows = slice((a * 2 + b) * block, (a * 2 + b + 1) * block)
                    cols = slice(n * inner, (n + 1) * inner)
                    qkv_ref[n, pl.ds(to, block), :] = src[rows, cols].astype(F32)
        at = pl.ds(pl.multiple_of(which * half_rows, half_rows), half_rows)
        for a in range(2):
            for b in range(2):
                rows = slice((a * 2 + b) * block, (a * 2 + b + 1) * block)
                to = slice((b * 2 + a) * block, (b * 2 + a + 1) * block)
                proj_ref[to, at] = src[rows, 3 * inner :].astype(F32)


def output_kernel(h1_ref, own_ref, recv_ref, bias_ref, out_ref):
    total = own_ref[...].astype(F32) + recv_ref[...].astype(F32)
    out_ref[...] = (h1_ref[...] + total + bias_ref[...]).astype(BF16)


def shape(dims, dtype):
    return jax.ShapeDtypeStruct(dims, dtype)


VMEM = functools.partial(pl.BlockSpec, memory_space=pltpu.VMEM)
SMEM = functools.partial(pl.BlockSpec, memory_space=pltpu.SMEM)


def swap(value, axis, size, bit):
    return lax.ppermute(value, axis, [(i, i ^ bit) for i in range(size)])


def add_pair(left, right):
    return left.astype(F32) + right.astype(F32)


def reduce_scatter(keep, send, bits, size):
    index = lax.axis_index("dp")
    for n, bit in enumerate(bits):
        recv = swap(send, "dp", size, bit)
        if n + 1 == len(bits):
            return add_pair(keep, recv).astype(BF16)
        rows = keep.shape[0] // 2
        upper = ((index & bits[n + 1]) != 0).astype(jnp.int32)

        def part(which):
            pick = lambda v: lax.dynamic_slice_in_dim(v, which * rows, rows, 0)
            return add_pair(pick(keep), pick(recv)).astype(BF16)

        keep, send = part(upper), part(1 - upper)


def gather_back(value, bits, size, ordered):
    index = lax.axis_index("dp")
    for bit in bits[:-1]:
        other = swap(value, "dp", size, bit)
        low, high = value, other
        if ordered:
            upper = (index & bit) != 0
            low, high = jnp.where(upper, other, value), jnp.where(upper, value, other)
        value = jnp.concatenate([low, high], axis=0)
    return value, swap(value, "dp", size, bits[-1])


def local(
    dp_size,
    inputs,
    ln1_gain,
    ln1_shift,
    w_qkv,
    qv_bias,
    bias_table,
    rel_index,
    regions,
    w_proj,
    proj_bias,
    ln2_gain,
    ln2_shift,
    w_fc1,
    fc1_bias,
    w_fc2,
    fc2_bias,
    grad_output,
):
    tokens, width = inputs.shape
    images = tokens // (SIDE * SIDE)
    inner = w_qkv.shape[2]
    heads = inner // HEAD_DIM
    lanes = heads * PAD
    wrows = WINDOWS * PAD
    srows = slab(0)[1]
    hidden = w_fc1.shape[1]
    table_rows = bias_table.shape[0]
    table_pad = -(-table_rows // 8) * 8
    row = lambda v: v.reshape(1, -1)

    def tensor_swap(value):
        return swap(value, "tensor", 2, 1)

    bits = [1 << n for n in range(dp_size.bit_length() - 1)]
    dp_index = lax.axis_index("dp").astype(jnp.int32).reshape(1)
    core_bit = dp_index & 1

    order = window_order()
    perms = []
    for image in range(images):
        offset = slab(image)[2]
        wide = ((0, 0), (offset, srows - offset - SIDE * SIDE))
        perms.append(jnp.asarray(np.pad(order, wide), BF16))
    shifted = jnp.asarray(window_order(0), BF16)
    group = jnp.asarray(np.kron(np.eye(heads, dtype=np.float32), np.ones((1, PAD), np.float32)))
    qkv_weight = w_qkv.transpose(1, 0, 2)

    masked_bias = pl.pallas_call(
        bias_kernel, out_shape=shape((wrows, lanes), F32), name="bias"
    )(bias_table.T, rel_index, row(regions), shifted)
    forward = []
    for image in range(images):
        outs = pl.pallas_call(
            functools.partial(attn_forward_kernel, image),
            out_shape=(
                shape((srows, width), BF16),
                shape((srows, width), BF16),
                shape((wrows, 3 * inner), BF16),
                shape((wrows, lanes), F32),
                shape((srows, inner), BF16),
            ),
            scratch_shapes=[pltpu.VMEM((wrows, inner), BF16)],
        )(
            inputs, row(ln1_gain), row(ln1_shift), qkv_weight, qv_bias, masked_bias, perms[image],
            w_proj,
        )
        forward.append(outs + (tensor_swap(outs[0]),))
    part0, n1a, qkvw0, prob0, otok0, recv0 = forward[0]
    part1, n1b, qkvw1, prob1, otok1, recv1 = forward[1]

    steps = hidden // HIDDEN_BLOCK
    full = lambda dims: pl.BlockSpec(dims, lambda j: (0, 0))
    cols = lambda rows: pl.BlockSpec((rows, HIDDEN_BLOCK), lambda j: (0, j))
    back_two_part, h1, n2, act, dub, grad_b1, grad_b2 = pl.pallas_call(
        mlp_kernel,
        grid=(steps,),
        in_specs=[
            full((tokens, width)), full((srows, width)), full((srows, width)),
            full((srows, width)), full((srows, width)), full((1, width)),
            full((1, width)), full((1, width)), cols(width), cols(1),
            pl.BlockSpec((HIDDEN_BLOCK, width), lambda j: (j, 0)), full((tokens, width)),
        ],
        out_specs=(
            full((tokens, width)), full((tokens, width)), full((tokens, width)), cols(tokens),
            cols(tokens), cols(1), full((1, width)),
        ),
        out_shape=(
            shape((tokens, width), BF16),
            shape((tokens, width), F32),
            shape((tokens, width), BF16),
            shape((tokens, hidden), BF16),
            shape((tokens, hidden), BF16),
            shape((1, hidden), F32),
            shape((1, width), F32),
        ),
        scratch_shapes=[pltpu.VMEM((tokens, width), F32)],
        name="mlp",
    )(
        inputs, part0, recv0, part1, recv1, row(proj_bias), row(ln2_gain), row(ln2_shift), w_fc1,
        row(fc1_bias), w_fc2, grad_output,
    )
    back_two_recv = tensor_swap(back_two_part)

    def mlp_grad(flip):
        return pl.pallas_call(
            functools.partial(mlp_grad_kernel, flip),
            in_specs=[SMEM()] + [VMEM()] * 4,
            out_shape=shape((hidden // 2, 2 * width), BF16),
        )(core_bit, act, dub, n2, grad_output)

    send = mlp_grad(1)
    keep = mlp_grad(0)
    mlp_shard = reduce_scatter(keep, send, bits, dp_size)
    mlp_part = pl.pallas_call(
        mlp_out_kernel, out_shape=shape((tokens, width), BF16), name="mlp_out"
    )(act, w_fc2)

    backward = []
    for image, (qkvw, prob) in enumerate(((qkvw0, prob0), (qkvw1, prob1))):
        outs = pl.pallas_call(
            functools.partial(attn_backward_kernel, image),
            out_shape=(
                shape((srows, width), BF16),
                shape((srows, width), F32),
                shape((srows, width), BF16),
                shape((srows, 3 * inner), BF16),
                shape((4, width), F32),
                shape((PAD, lanes), F32),
            ),
            scratch_shapes=[
                pltpu.VMEM((wrows, inner), BF16),
                pltpu.VMEM((wrows, 3 * inner), BF16),
            ],
        )(
            grad_output, back_two_part, back_two_recv, h1, row(ln2_gain), w_proj, qkvw, prob,
            perms[image], qkv_weight,
        )
        backward.append(outs + (tensor_swap(outs[0]),))
    back0, dh0, dhb0, dp0, sums0, dsum0, back_recv0 = backward[0]
    back1, dh1, dhb1, dp1, sums1, dsum1, back_recv1 = backward[1]

    def attn_grad(flip):
        return pl.pallas_call(
            functools.partial(attn_grad_kernel, flip),
            in_specs=[SMEM()] + [VMEM()] * 8,
            out_shape=shape((width // 2, 3 * inner + inner), BF16),
        )(core_bit, n1a, n1b, dp0, dp1, otok0, otok1, dhb0, dhb1)

    send = attn_grad(1)
    keep = attn_grad(0)
    attn_shard = reduce_scatter(keep, send, bits, dp_size)

    table_sum = pl.pallas_call(
        table_kernel,
        out_shape=shape((heads, table_pad), F32),
        scratch_shapes=[pltpu.VMEM((table_pad, lanes), F32), pltpu.VMEM((PAD, lanes), F32)],
        name="table",
    )(dsum0, dsum1, rel_index, group)

    mlp_recv = tensor_swap(mlp_part)
    output = pl.pallas_call(
        output_kernel, out_shape=shape((tokens, width), BF16), name="output"
    )(h1, mlp_part, mlp_recv, row(fc2_bias))

    small_rows = 7 + hidden // width + heads
    grad_input, small = pl.pallas_call(
        input_grad_kernel,
        out_shape=(shape((tokens, width), F32), shape((small_rows, width), F32)),
        name="input_grad",
    )(
        inputs, back0, back_recv0, back1, back_recv1, dh0, dh1, row(ln1_gain), sums0, sums1,
        grad_b1, grad_b2, table_sum,
    )
    for n, bit in enumerate(bits):
        recv = swap(small, "dp", dp_size, bit)
        if n + 1 < len(bits):
            small = small + recv
    smalls = pl.pallas_call(
        small_kernel,
        out_shape=tuple(shape((1, width), F32) for _ in range(5))
        + (
            shape((2, inner), F32),
            shape((1, width), F32),
            shape((1, hidden), F32),
            shape((heads, table_rows), F32),
        ),
        name="small",
    )(small, recv)
    grad_gain1, grad_shift1, grad_gain2, grad_shift2, grad_pb, grad_qvb, grad_b2, grad_b1 = smalls[:8]

    down = bits[::-1]
    mine, other = gather_back(mlp_shard, down, dp_size, False)
    grad_fc2, grad_fc1 = pl.pallas_call(
        functools.partial(mlp_finish_kernel, down[:-1]),
        in_specs=[SMEM()] + [VMEM()] * 2,
        out_shape=(shape((hidden, width), F32), shape((width, hidden), F32)),
        name="mlp_finish",
    )(dp_index, mine, other)
    mine, other = gather_back(attn_shard, down[:-3] + [down[-2], down[-3], down[-1]], dp_size, True)
    grad_qkv, grad_proj = pl.pallas_call(
        attn_finish_kernel,
        in_specs=[SMEM()] + [VMEM()] * 2,
        out_shape=(shape((3, width, inner), F32), shape((inner, width), F32)),
        name="attn_finish",
    )(core_bit, mine, other)

    flat = lambda v: v.reshape(-1)
    return (
        output, grad_input, flat(grad_gain1), flat(grad_shift1), grad_qkv.transpose(1, 0, 2),
        grad_qvb, smalls[8].T, grad_proj, flat(grad_pb), flat(grad_gain2), flat(grad_shift2),
        grad_fc1, flat(grad_b1), grad_fc2, flat(grad_b2),
    )


def solution(mesh):
    size = mesh.shape["dp"]

    def body(*args):
        return local(size, *args)

    return jax.shard_map(
        body,
        mesh=mesh,
        in_specs=(
            P("dp", None),
            P(),
            P(),
            P(None, None, "tensor"),
            P(None, "tensor"),
            P(None, "tensor"),
            P(),
            P(),
            P("tensor", None),
            P(),
            P(),
            P(),
            P(None, "tensor"),
            P("tensor"),
            P("tensor", None),
            P(),
            P("dp", None),
        ),
        out_specs=(
            P("dp", None),
            P("dp", None),
            P(),
            P(),
            P(None, None, "tensor"),
            P(None, "tensor"),
            P(None, "tensor"),
            P("tensor", None),
            P(),
            P(),
            P(),
            P(None, "tensor"),
            P("tensor"),
            P("tensor", None),
            P(),
        ),
        check_vma=False,
    )
```

```python
import functools

import numpy as np
import jax
import jax.numpy as jnp
from jax import lax
from jax.experimental import pallas as pl
from jax.experimental.pallas import tpu as pltpu
from jax.sharding import PartitionSpec as P

HEAD_DIM = 32
SIDE = 14
WIN = 7
SHIFT = 3
ACROSS = SIDE // WIN
POSITIONS = WIN * WIN
PAD = 64
WINDOWS = ACROSS * ACROSS

NORM_EPS = 1e-05
MASKED = -1e30
F32 = jnp.float32
BF16 = jnp.bfloat16
HIDDEN_BLOCK = 256


def dot(a, b, dims=((1,), (0,)), precision=None):
    return lax.dot_general(a, b, (dims, ((), ())), preferred_element_type=F32, precision=precision)


NT = ((1,), (1,))
TN = ((0,), (0,))


def normed(values):
    centered = values - jnp.mean(values, axis=-1, keepdims=True)
    inverse = lax.rsqrt(jnp.mean(centered * centered, axis=-1, keepdims=True) + NORM_EPS)
    return centered * inverse, inverse


def norm_backward(upstream, unit, inverse, gain):
    weighted = upstream * gain
    return inverse * (
        weighted
        - jnp.mean(weighted, axis=-1, keepdims=True)
        - unit * jnp.mean(weighted * unit, axis=-1, keepdims=True)
    )


def window_order(shift=SHIFT):
    order = np.zeros((WINDOWS * PAD, SIDE * SIDE), np.float32)
    for a in range(ACROSS):
        for b in range(ACROSS):
            for i in range(POSITIONS):
                row = (a * WIN + i // WIN + shift) % SIDE
                col = (b * WIN + i % WIN + shift) % SIDE
                order[(a * ACROSS + b) * PAD + i, row * SIDE + col] = 1.0
    return order


GROUP = 128 // HEAD_DIM


def head_lanes(dtype):
    lane = lax.broadcasted_iota(jnp.int32, (PAD, 128), 1) // HEAD_DIM
    return [(lane == h).astype(dtype) for h in range(GROUP)]


def spread_heads(tile, masks):
    return jnp.concatenate([tile * mask for mask in masks], axis=0)


def gather_heads(full):
    lane = lax.broadcasted_iota(jnp.int32, (PAD, 128), 1) // HEAD_DIM
    total = full[:PAD, :]
    for h in range(1, GROUP):
        total = jnp.where(lane == h, full[h * PAD : (h + 1) * PAD, :], total)
    return total


def slab(image):
    start = image * SIDE * SIDE // 8 * 8
    return start, -(-SIDE * SIDE // 8) * 8, image * SIDE * SIDE - start


def own_rows(image, rows):
    offset = slab(image)[2]
    at = lax.broadcasted_iota(jnp.int32, (rows, 1), 0)
    return ((at >= offset) & (at < offset + SIDE * SIDE)).astype(F32)


def pair_index(rel_ref):
    lane = lax.broadcasted_iota(jnp.int32, (POSITIONS, 2 * PAD), 1)
    sub = lax.broadcasted_iota(jnp.int32, (POSITIONS, 2 * PAD), 0)
    same = (lax.rem(lane, PAD) == sub).astype(BF16)
    spread = dot((rel_ref[...] + 1).astype(F32).astype(BF16), same, TN)
    zero = jnp.zeros((PAD - POSITIONS, 2 * PAD), F32)
    return jnp.concatenate([spread, zero], axis=0).astype(jnp.int32)


def bias_kernel(index_ref, table_ref, rel_ref, reg_ref, order_ref, bm_ref):
    heads, entries = table_ref.shape
    index = pair_index(rel_ref) - 1
    first = jnp.clip(index, 0, 127)
    second = jnp.clip(index - 128, 0, 127)
    left = lax.broadcasted_iota(jnp.int32, index.shape, 1) < PAD

    def pick(h):
        low = jnp.broadcast_to(table_ref[h : h + 1, :128], index.shape)
        high = jnp.concatenate(
            [table_ref[h : h + 1, 128:], jnp.zeros((1, 256 - entries), F32)], axis=1
        )
        high = jnp.broadcast_to(high, index.shape)
        return jnp.where(
            index < 128,
            jnp.take_along_axis(low, first, axis=1),
            jnp.take_along_axis(high, second, axis=1),
        )

    region = jnp.broadcast_to((reg_ref[...] + 1).astype(F32), (16, reg_ref.shape[1])).astype(BF16)
    order = order_ref[...]
    across = dot(region, order, NT)
    down = dot(order, region, NT)
    hits = []
    for w in range(WINDOWS):
        rows = slice(w * PAD, (w + 1) * PAD)
        hits.append(down[rows, 0:1] == jnp.concatenate([across[0:1, rows]] * 2, axis=1))
    for p in range(heads // 2):
        bias = jnp.where(left, pick(2 * p), pick(2 * p + 1))
        for w in range(WINDOWS):
            rows = slice(w * PAD, (w + 1) * PAD)
            bm_ref[rows, p * 128 : (p + 1) * 128] = jnp.where(hits[w], bias, MASKED)


def attn_forward_kernel(
    image, x_ref, gain_ref, shift_ref, wqkv_ref, qvb_ref, bm_ref, perm_ref, wproj_ref,
    part_ref, n1_ref, qkvw_ref, prob_ref, otok_ref,
    ow_ref,
):
    inner = wproj_ref.shape[0]
    start, size, _ = slab(image)
    unit, _ = normed(x_ref[start : start + size, :].astype(F32))
    n1 = (unit * gain_ref[...] + shift_ref[...]).astype(BF16)
    n1_ref[...] = n1
    q = ((dot(n1, wqkv_ref[0]) + qvb_ref[0:1, :]) * (HEAD_DIM ** (-0.5))).astype(BF16)
    k = dot(n1, wqkv_ref[1]).astype(BF16)
    v = (dot(n1, wqkv_ref[2]) + qvb_ref[1:2, :]).astype(BF16)
    perm = perm_ref[...]
    qkvw_ref[:, :inner] = dot(perm, q).astype(BF16)
    qkvw_ref[:, inner : 2 * inner] = dot(perm, k).astype(BF16)
    qkvw_ref[:, 2 * inner :] = dot(perm, v).astype(BF16)

    def window(i, carry):
        rows = pl.ds(pl.multiple_of(i * PAD, PAD), PAD)
        masks = head_lanes(BF16)
        for g in range(inner // 128):
            cols = slice(g * 128, (g + 1) * 128)
            wide = slice(g * GROUP * PAD, (g + 1) * GROUP * PAD)
            at = lambda n: slice(n * inner + g * 128, n * inner + (g + 1) * 128)
            spread = spread_heads(qkvw_ref[rows, at(0)], masks)
            s = dot(qkvw_ref[rows, at(1)], spread, NT) + bm_ref[rows, wide]
            e = jnp.exp(s - jnp.max(s, axis=0, keepdims=True))
            p = e * (1.0 / jnp.sum(e, axis=0, keepdims=True))
            prob_ref[rows, wide] = p
            full = dot(p.astype(BF16), qkvw_ref[rows, at(2)], TN)
            ow_ref[rows, cols] = gather_heads(full).astype(BF16)
        return carry

    lax.fori_loop(0, WINDOWS, window, 0)
    otok = dot(perm, ow_ref[...], TN).astype(BF16)
    otok_ref[...] = otok
    part_ref[...] = dot(otok, wproj_ref[...]).astype(BF16)


def mlp_kernel(
    x_ref, own0_ref, recv0_ref, own1_ref, recv1_ref, pbias_ref, gain_ref, shift_ref, w1_ref,
    b1_ref, w2_ref, dy_ref,
    back_ref, h1_ref, n2_ref, act_ref, dub_ref, gb1_ref, gb2_ref,
    acc_ref,
):
    step = pl.program_id(0)

    @pl.when(step == 0)
    def _():
        h1_ref[...] = x_ref[...].astype(F32) + pbias_ref[...]
        for image, (own, recv) in enumerate(((own0_ref, recv0_ref), (own1_ref, recv1_ref))):
            start, size, _ = slab(image)
            total = own[...].astype(F32) + recv[...].astype(F32)
            h1_ref[start : start + size, :] += total
        unit, _ = normed(h1_ref[...])
        n2_ref[...] = (unit * gain_ref[...] + shift_ref[...]).astype(BF16)
        gb2_ref[...] = jnp.sum(dy_ref[...].astype(F32), axis=0, keepdims=True)
        acc_ref[...] = jnp.zeros_like(acc_ref)

    u = dot(n2_ref[...], w1_ref[...]) + b1_ref[...]
    cdf = 0.5 * (1.0 + lax.erf(u * 0.7071067811865476))
    act_ref[...] = (u * cdf).astype(BF16)
    slope = cdf + u * jnp.exp(-0.5 * u * u) * 0.3989422804014327
    du = dot(dy_ref[...], w2_ref[...], NT) * slope
    gb1_ref[...] = jnp.sum(du, axis=0, keepdims=True)
    dub = du.astype(BF16)
    dub_ref[...] = dub
    acc_ref[...] += dot(dub, w1_ref[...], NT)

    @pl.when(step == pl.num_programs(0) - 1)
    def _():
        back_ref[...] = acc_ref[...].astype(BF16)


def half(ref, which, size):
    return ref[:, pl.ds(pl.multiple_of(which * size, size), size)]


def mlp_grad_kernel(flip, index_ref, act_ref, dub_ref, n2_ref, dy_ref, out_ref):
    which = (index_ref[0] & 1) ^ flip
    size = act_ref.shape[1] // 2
    width = dy_ref.shape[1]
    out_ref[:, :width] = dot(half(act_ref, which, size), dy_ref[...], TN).astype(BF16)
    out_ref[:, width:] = dot(n2_ref[...], half(dub_ref, which, size), TN).astype(BF16)


def mlp_out_kernel(act_ref, w2_ref, part_ref):
    part_ref[...] = dot(act_ref[...], w2_ref[...]).astype(BF16)


def attn_backward_kernel(
    image, dy_ref, own_ref, recv_ref, h1_ref, gain_ref, wproj_ref, qkvw_ref, prob_ref, perm_ref,
    wqkv_ref,
    part_ref, dh_ref, dhb_ref, dp_ref, sums_ref, dsum_ref,
    dow_ref, dqkv_ref,
):
    inner = wproj_ref.shape[0]
    start, size, _ = slab(image)
    slab_rows = slice(start, start + size)
    mask = own_rows(image, size)
    dn2 = own_ref[slab_rows, :].astype(F32) + recv_ref[slab_rows, :].astype(F32)
    unit, inverse = normed(h1_ref[slab_rows, :])
    mine = dn2 * mask
    sums_ref[0:1, :] = jnp.sum(mine * unit, axis=0, keepdims=True)
    sums_ref[1:2, :] = jnp.sum(mine, axis=0, keepdims=True)
    dh = dy_ref[slab_rows, :].astype(F32) + norm_backward(dn2, unit, inverse, gain_ref[...])
    dh_ref[...] = dh
    sums_ref[2:3, :] = jnp.sum(dh * mask, axis=0, keepdims=True)
    dhb = dh.astype(BF16)
    dhb_ref[...] = dhb
    perm = perm_ref[...]
    dow_ref[...] = dot(perm, dot(dhb, wproj_ref[...], NT).astype(BF16)).astype(BF16)
    dsum_ref[...] = jnp.zeros_like(dsum_ref)
    groups = inner // 128

    def window(i, carry):
        rows = pl.ds(pl.multiple_of(i * PAD, PAD), PAD)
        masks = head_lanes(BF16)
        sums = []
        for g in range(groups):
            wide = slice(g * GROUP * PAD, (g + 1) * GROUP * PAD)
            at = lambda n: slice(n * inner + g * 128, n * inner + (g + 1) * 128)
            qblk = spread_heads(qkvw_ref[rows, at(0)], masks)
            oblk = spread_heads(dow_ref[rows, at(0)], masks)
            p = prob_ref[rows, wide]
            dp = dot(qkvw_ref[rows, at(2)], oblk, NT)
            ds = p * (dp - jnp.sum(p * dp, axis=0, keepdims=True))
            dsum_ref[:, wide] += ds
            dsb = ds.astype(BF16)
            dq = gather_heads(dot(dsb, qkvw_ref[rows, at(1)], TN)) * (HEAD_DIM ** (-0.5))
            dv = dot(p.astype(BF16), oblk)
            dqkv_ref[rows, at(0)] = dq.astype(BF16)
            dqkv_ref[rows, at(1)] = dot(dsb, qblk).astype(BF16)
            dqkv_ref[rows, at(2)] = dv.astype(BF16)
            sums += [jnp.sum(dq, axis=0, keepdims=True), jnp.sum(dv, axis=0, keepdims=True)]
        return tuple(a + b for a, b in zip(carry, sums))

    zero = jnp.zeros((1, 128), F32)
    sums = lax.fori_loop(0, WINDOWS, window, (zero,) * (2 * groups))
    for g in range(groups):
        sums_ref[3:4, g * 128 : (g + 1) * 128] = sums[2 * g]
        sums_ref[3:4, inner + g * 128 : inner + (g + 1) * 128] = sums[2 * g + 1]
    dp_tok = dot(perm, dqkv_ref[...], TN).astype(BF16)
    dp_ref[...] = dp_tok
    part = dot(dp_tok[:, :inner], wqkv_ref[0], NT)
    part = part + dot(dp_tok[:, inner : 2 * inner], wqkv_ref[1], NT)
    part_ref[...] = (part + dot(dp_tok[:, 2 * inner :], wqkv_ref[2], NT)).astype(BF16)


def attn_grad_kernel(
    flip, index_ref, n1a_ref, n1b_ref, dpa_ref, dpb_ref, oa_ref, ob_ref, dha_ref, dhb_ref, out_ref
):
    which = (index_ref[0] & 1) ^ flip
    wide = dpa_ref.shape[1]
    rows = n1a_ref.shape[1] // 2
    qkv = dot(half(n1a_ref, which, rows), dpa_ref[...], TN)
    out_ref[:, :wide] = (qkv + dot(half(n1b_ref, which, rows), dpb_ref[...], TN)).astype(BF16)
    proj = dot(oa_ref[...], half(dha_ref, which, rows), TN)
    out_ref[:, wide:] = (proj + dot(ob_ref[...], half(dhb_ref, which, rows), TN)).astype(BF16)


def table_kernel(dsa_ref, dsb_ref, rel_ref, group_ref, out_ref, tab_ref, dsum_ref):
    rel = pair_index(rel_ref)
    width = rel.shape[1]
    pairs = dsum_ref.shape[1] // width
    dsum_ref[...] = dsa_ref[...] + dsb_ref[...]

    def eight(n, carry):
        for p in range(pairs):
            cols = slice(p * width, (p + 1) * width)
            part = dsum_ref[:, cols]
            found = [
                jnp.sum(jnp.where(rel == n * 8 + t + 1, part, 0.0), axis=0, keepdims=True)
                for t in range(8)
            ]
            tab_ref[pl.ds(pl.multiple_of(n * 8, 8), 8), cols] = jnp.concatenate(found, axis=0)
        return carry

    lax.fori_loop(0, tab_ref.shape[0] // 8, eight, 0)
    out_ref[...] = dot(group_ref[...], tab_ref[...], NT, lax.Precision.HIGHEST)


def input_grad_kernel(
    x_ref, own0_ref, recv0_ref, own1_ref, recv1_ref, dh0_ref, dh1_ref, gain_ref,
    sums0_ref, sums1_ref, gb1_ref, gb2_ref, tab_ref,
    gin_ref, small_ref,
):
    width = x_ref.shape[1]
    small_ref[...] = jnp.zeros_like(small_ref)
    for image, (own, recv, dh) in enumerate(
        ((own0_ref, recv0_ref, dh0_ref), (own1_ref, recv1_ref, dh1_ref))
    ):
        start, size, offset = slab(image)
        unit, inverse = normed(x_ref[start : start + size, :].astype(F32))
        dn1 = own[...].astype(F32) + recv[...].astype(F32)
        small_ref[0:1, :] += jnp.sum(dn1 * unit, axis=0, keepdims=True)
        small_ref[1:2, :] += jnp.sum(dn1, axis=0, keepdims=True)
        gin = dh[...] + norm_backward(dn1, unit, inverse, gain_ref[...])
        if offset == 0:
            gin_ref[start : start + size, :] = gin
        else:
            at = lax.broadcasted_iota(jnp.int32, (8, 1), 0)
            gin_ref[start : start + 8, :] = jnp.where(
                at < offset, gin_ref[start : start + 8, :], gin[:8, :]
            )
            gin_ref[start + 8 : start + size, :] = gin[8:, :]
    small_ref[2:6, :] = sums0_ref[...] + sums1_ref[...]
    small_ref[6:7, :] = gb2_ref[...]
    at = 7
    for n in range(gb1_ref.shape[1] // width):
        small_ref[at : at + 1, :] = gb1_ref[:, n * width : (n + 1) * width]
        at += 1
    for h in range(tab_ref.shape[0]):
        small_ref[at : at + 1, : tab_ref.shape[1]] = tab_ref[h : h + 1, :]
        at += 1


def small_kernel(
    left_ref, right_ref,
    gain1_ref, shift1_ref, gain2_ref, shift2_ref, pbias_ref, qvb_ref, gb2_ref, gb1_ref, tab_ref,
):
    small = left_ref[...] + right_ref[...]
    width = small.shape[1]
    inner = qvb_ref.shape[1]
    for n, out in enumerate((gain1_ref, shift1_ref, gain2_ref, shift2_ref, pbias_ref)):
        out[...] = small[n : n + 1, :]
    qvb_ref[0:1, :] = small[5:6, :inner]
    qvb_ref[1:2, :] = small[5:6, inner:]
    gb2_ref[...] = small[6:7, :]
    at = 7
    for n in range(gb1_ref.shape[1] // width):
        gb1_ref[:, n * width : (n + 1) * width] = small[at : at + 1, :]
        at += 1
    tab_ref[...] = small[at : at + tab_ref.shape[0], : tab_ref.shape[1]]


def mlp_finish_kernel(index_ref, mine_ref, other_ref, fc2_ref, fc1_ref):
    rows, width = mine_ref.shape[0], fc2_ref.shape[1]
    for src, which in ((mine_ref, index_ref[0] & 1), (other_ref, 1 - (index_ref[0] & 1))):
        at = pl.ds(pl.multiple_of(which * rows, rows), rows)
        fc2_ref[at, :] = src[:, :width].astype(F32)
        fc1_ref[:, at] = src[:, width:].astype(F32)


def split_kernel(place, index_ref, keep_ref, recv_ref, kept_ref, send_ref):
    rows = kept_ref.shape[0]
    upper = lax.shift_right_logical(index_ref[0], place) & 1
    for out, which in ((send_ref, 1 - upper), (kept_ref, upper)):
        at = pl.ds(pl.multiple_of(which * rows, rows), rows)
        out[...] = add_pair(keep_ref[at, :], recv_ref[at, :]).astype(BF16)


def sum_kernel(left_ref, right_ref, out_ref):
    out_ref[...] = add_pair(left_ref[...], right_ref[...]).astype(out_ref.dtype)


def join_kernel(place, index_ref, mine_ref, other_ref, out_ref):
    rows = mine_ref.shape[0]
    upper = lax.shift_right_logical(index_ref[0], place) & 1
    out_ref[pl.ds(pl.multiple_of(upper * rows, rows), rows), :] = mine_ref[...]
    out_ref[pl.ds(pl.multiple_of((1 - upper) * rows, rows), rows), :] = other_ref[...]


def attn_finish_kernel(index_ref, mine_ref, other_ref, qkv_ref, proj_ref):
    inner = qkv_ref.shape[2]
    half_rows = qkv_ref.shape[1] // 2
    block = half_rows // 4
    for src, which in ((mine_ref, index_ref[0] & 1), (other_ref, 1 - (index_ref[0] & 1))):
        for n in range(3):
            for a in range(2):
                for b in range(2):
                    to = pl.multiple_of(which * half_rows + (b * 2 + a) * block, block)
                    rows = slice((a * 2 + b) * block, (a * 2 + b + 1) * block)
                    cols = slice(n * inner, (n + 1) * inner)
                    qkv_ref[n, pl.ds(to, block), :] = src[rows, cols].astype(F32)
        at = pl.ds(pl.multiple_of(which * half_rows, half_rows), half_rows)
        for a in range(2):
            for b in range(2):
                rows = slice((a * 2 + b) * block, (a * 2 + b + 1) * block)
                to = slice((b * 2 + a) * block, (b * 2 + a + 1) * block)
                proj_ref[to, at] = src[rows, 3 * inner :].astype(F32)


def output_kernel(h1_ref, own_ref, recv_ref, bias_ref, out_ref):
    total = own_ref[...].astype(F32) + recv_ref[...].astype(F32)
    out_ref[...] = (h1_ref[...] + total + bias_ref[...]).astype(BF16)


def shape(dims, dtype):
    return jax.ShapeDtypeStruct(dims, dtype)


VMEM = functools.partial(pl.BlockSpec, memory_space=pltpu.VMEM)
SMEM = functools.partial(pl.BlockSpec, memory_space=pltpu.SMEM)
PARAMS = pltpu.CompilerParams(vmem_limit_bytes=12 << 20)


def call(kernel, out_shape, scratch=(), smem=0):
    def run(*args):
        return pl.pallas_call(
            kernel,
            in_specs=[SMEM()] * smem + [VMEM()] * (len(args) - smem),
            out_shape=out_shape,
            scratch_shapes=list(scratch),
            compiler_params=PARAMS,
        )(*args)

    return run


def swap(value, axis, size, bit):
    return lax.ppermute(value, axis, [(i, i ^ bit) for i in range(size)])


def add_pair(left, right):
    return left.astype(F32) + right.astype(F32)


def reduce_scatter(keep, send, bits, size, index):
    for n, bit in enumerate(bits):
        recv = swap(send, "dp", size, bit)
        if n + 1 == len(bits):
            return call(sum_kernel, shape(keep.shape, BF16))(keep, recv)
        rows = keep.shape[0] // 2
        place = bits[n + 1].bit_length() - 1
        half_shape = shape((rows, keep.shape[1]), BF16)
        if rows % 16 == 0:
            keep, send = call(
                functools.partial(split_kernel, place),
                (half_shape, half_shape), smem=1,
            )(index, keep, recv)
        else:
            upper = ((index[0] >> place) & 1) != 0
            total = add_pair(keep, recv).astype(BF16)
            low, high = total[:rows], total[rows:]
            keep, send = jnp.where(upper, high, low), jnp.where(upper, low, high)


def gather_back(value, bits, size, index):
    for bit in bits[:-1]:
        other = swap(value, "dp", size, bit)
        rows = value.shape[0]
        place = bit.bit_length() - 1
        if rows % 16 == 0:
            value = call(
                functools.partial(join_kernel, place),
                shape((2 * rows, value.shape[1]), BF16), smem=1,
            )(index, value, other)
        else:
            upper = ((index[0] >> place) & 1) != 0
            low, high = jnp.where(upper, other, value), jnp.where(upper, value, other)
            value = jnp.concatenate([low, high], axis=0)
    return value, swap(value, "dp", size, bits[-1])


def local(
    dp_size,
    inputs,
    ln1_gain,
    ln1_shift,
    w_qkv,
    qv_bias,
    bias_table,
    rel_index,
    regions,
    w_proj,
    proj_bias,
    ln2_gain,
    ln2_shift,
    w_fc1,
    fc1_bias,
    w_fc2,
    fc2_bias,
    grad_output,
):
    tokens, width = inputs.shape
    images = tokens // (SIDE * SIDE)
    inner = w_qkv.shape[2]
    heads = inner // HEAD_DIM
    lanes = heads * PAD
    wrows = WINDOWS * PAD
    srows = slab(0)[1]
    hidden = w_fc1.shape[1]
    table_rows = bias_table.shape[0]
    table_pad = -(-table_rows // 8) * 8
    row = lambda v: v.reshape(1, -1)

    def tensor_swap(value):
        return swap(value, "tensor", 2, 1)

    bits = [1 << n for n in range(dp_size.bit_length() - 1)]
    dp_index = lax.axis_index("dp").astype(jnp.int32).reshape(1)

    order = window_order()
    perms = []
    for image in range(images):
        offset = slab(image)[2]
        wide = ((0, 0), (offset, srows - offset - SIDE * SIDE))
        perms.append(jnp.asarray(np.pad(order, wide), BF16))
    shifted = jnp.asarray(window_order(0), BF16)
    group = jnp.asarray(np.kron(np.eye(heads, dtype=np.float32), np.ones((1, PAD), np.float32)))
    qkv_weight = w_qkv.transpose(1, 0, 2)

    masked_bias = call(bias_kernel, shape((wrows, lanes), F32), smem=1)(
        dp_index, bias_table.T, rel_index, row(regions), shifted
    )
    forward = []
    for image in range(images):
        outs = pl.pallas_call(
            functools.partial(attn_forward_kernel, image),
            out_shape=(
                shape((srows, width), BF16),
                shape((srows, width), BF16),
                shape((wrows, 3 * inner), BF16),
                shape((wrows, lanes), F32),
                shape((srows, inner), BF16),
            ),
            scratch_shapes=[pltpu.VMEM((wrows, inner), BF16)],
            compiler_params=PARAMS,
        )(
            inputs, row(ln1_gain), row(ln1_shift), qkv_weight, qv_bias, masked_bias, perms[image],
            w_proj,
        )
        forward.append(outs + (tensor_swap(outs[0]),))
    part0, n1a, qkvw0, prob0, otok0, recv0 = forward[0]
    part1, n1b, qkvw1, prob1, otok1, recv1 = forward[1]

    steps = hidden // HIDDEN_BLOCK
    full = lambda dims: pl.BlockSpec(dims, lambda j: (0, 0))
    cols = lambda rows: pl.BlockSpec((rows, HIDDEN_BLOCK), lambda j: (0, j))
    back_two_part, h1, n2, act, dub, grad_b1, grad_b2 = pl.pallas_call(
        mlp_kernel,
        grid=(steps,),
        in_specs=[
            full((tokens, width)), full((srows, width)), full((srows, width)),
            full((srows, width)), full((srows, width)), full((1, width)),
            full((1, width)), full((1, width)), cols(width), cols(1),
            pl.BlockSpec((HIDDEN_BLOCK, width), lambda j: (j, 0)), full((tokens, width)),
        ],
        out_specs=(
            full((tokens, width)), full((tokens, width)), full((tokens, width)), cols(tokens),
            cols(tokens), cols(1), full((1, width)),
        ),
        out_shape=(
            shape((tokens, width), BF16),
            shape((tokens, width), F32),
            shape((tokens, width), BF16),
            shape((tokens, hidden), BF16),
            shape((tokens, hidden), BF16),
            shape((1, hidden), F32),
            shape((1, width), F32),
        ),
        scratch_shapes=[pltpu.VMEM((tokens, width), F32)],
        compiler_params=PARAMS,
        name="mlp",
    )(
        inputs, part0, recv0, part1, recv1, row(proj_bias), row(ln2_gain), row(ln2_shift), w_fc1,
        row(fc1_bias), w_fc2, grad_output,
    )
    back_two_recv = tensor_swap(back_two_part)

    def mlp_grad(flip):
        return pl.pallas_call(
            functools.partial(mlp_grad_kernel, flip),
            in_specs=[SMEM()] + [VMEM()] * 4,
            out_shape=shape((hidden // 2, 2 * width), BF16),
            compiler_params=PARAMS,
        )(dp_index, act, dub, n2, grad_output)

    send = mlp_grad(1)
    keep = mlp_grad(0)
    mlp_shard = reduce_scatter(keep, send, bits, dp_size, dp_index)
    mlp_part = pl.pallas_call(
        mlp_out_kernel, out_shape=shape((tokens, width), BF16), compiler_params=PARAMS, name="mlp_out"
    )(act, w_fc2)

    backward = []
    for image, (qkvw, prob) in enumerate(((qkvw0, prob0), (qkvw1, prob1))):
        outs = pl.pallas_call(
            functools.partial(attn_backward_kernel, image),
            out_shape=(
                shape((srows, width), BF16),
                shape((srows, width), F32),
                shape((srows, width), BF16),
                shape((srows, 3 * inner), BF16),
                shape((4, width), F32),
                shape((PAD, lanes), F32),
            ),
            scratch_shapes=[
                pltpu.VMEM((wrows, inner), BF16),
                pltpu.VMEM((wrows, 3 * inner), BF16),
            ],
            compiler_params=PARAMS,
        )(
            grad_output, back_two_part, back_two_recv, h1, row(ln2_gain), w_proj, qkvw, prob,
            perms[image], qkv_weight,
        )
        backward.append(outs + (tensor_swap(outs[0]),))
    back0, dh0, dhb0, dp0, sums0, dsum0, back_recv0 = backward[0]
    back1, dh1, dhb1, dp1, sums1, dsum1, back_recv1 = backward[1]

    def attn_grad(flip):
        return pl.pallas_call(
            functools.partial(attn_grad_kernel, flip),
            in_specs=[SMEM()] + [VMEM()] * 8,
            out_shape=shape((width // 2, 3 * inner + inner), BF16),
            compiler_params=PARAMS,
        )(dp_index, n1a, n1b, dp0, dp1, otok0, otok1, dhb0, dhb1)

    send = attn_grad(1)
    keep = attn_grad(0)
    attn_shard = reduce_scatter(keep, send, bits, dp_size, dp_index)

    table_sum = pl.pallas_call(
        table_kernel,
        out_shape=shape((heads, table_pad), F32),
        scratch_shapes=[pltpu.VMEM((table_pad, lanes), F32), pltpu.VMEM((PAD, lanes), F32)],
        compiler_params=PARAMS,
        name="table",
    )(dsum0, dsum1, rel_index, group)

    mlp_recv = tensor_swap(mlp_part)
    output = pl.pallas_call(
        output_kernel, out_shape=shape((tokens, width), BF16), compiler_params=PARAMS, name="output"
    )(h1, mlp_part, mlp_recv, row(fc2_bias))

    small_rows = 7 + hidden // width + heads
    grad_input, small = pl.pallas_call(
        input_grad_kernel,
        out_shape=(shape((tokens, width), F32), shape((small_rows, width), F32)),
        compiler_params=PARAMS,
        name="input_grad",
    )(
        inputs, back0, back_recv0, back1, back_recv1, dh0, dh1, row(ln1_gain), sums0, sums1,
        grad_b1, grad_b2, table_sum,
    )
    for n, bit in enumerate(bits):
        recv = swap(small, "dp", dp_size, bit)
        if n + 1 < len(bits):
            small = small + recv
    smalls = pl.pallas_call(
        small_kernel,
        out_shape=tuple(shape((1, width), F32) for _ in range(5))
        + (
            shape((2, inner), F32),
            shape((1, width), F32),
            shape((1, hidden), F32),
            shape((heads, table_rows), F32),
        ),
        compiler_params=PARAMS,
        name="small",
    )(small, recv)
    grad_gain1, grad_shift1, grad_gain2, grad_shift2, grad_pb, grad_qvb, grad_b2, grad_b1 = smalls[:8]

    down = bits[::-1]
    mine, other = gather_back(mlp_shard, down, dp_size, dp_index)
    grad_fc2, grad_fc1 = pl.pallas_call(
        mlp_finish_kernel,
        in_specs=[SMEM()] + [VMEM()] * 2,
        out_shape=(shape((hidden, width), F32), shape((width, hidden), F32)),
        compiler_params=PARAMS,
        name="mlp_finish",
    )(dp_index, mine, other)
    mine, other = gather_back(
        attn_shard, down[:-3] + [down[-2], down[-3], down[-1]], dp_size, dp_index
    )
    grad_qkv, grad_proj = pl.pallas_call(
        attn_finish_kernel,
        in_specs=[SMEM()] + [VMEM()] * 2,
        out_shape=(shape((3, width, inner), F32), shape((inner, width), F32)),
        compiler_params=PARAMS,
        name="attn_finish",
    )(dp_index, mine, other)

    flat = lambda v: v.reshape(-1)
    return (
        output, grad_input, flat(grad_gain1), flat(grad_shift1), grad_qkv.transpose(1, 0, 2),
        grad_qvb, smalls[8].T, grad_proj, flat(grad_pb), flat(grad_gain2), flat(grad_shift2),
        grad_fc1, flat(grad_b1), grad_fc2, flat(grad_b2),
    )


def solution(mesh):
    size = mesh.shape["dp"]

    def body(*args):
        return local(size, *args)

    return jax.shard_map(
        body,
        mesh=mesh,
        in_specs=(
            P("dp", None),
            P(),
            P(),
            P(None, None, "tensor"),
            P(None, "tensor"),
            P(None, "tensor"),
            P(),
            P(),
            P("tensor", None),
            P(),
            P(),
            P(),
            P(None, "tensor"),
            P("tensor"),
            P("tensor", None),
            P(),
            P("dp", None),
        ),
        out_specs=(
            P("dp", None),
            P("dp", None),
            P(),
            P(),
            P(None, None, "tensor"),
            P(None, "tensor"),
            P(None, "tensor"),
            P("tensor", None),
            P(),
            P(),
            P(),
            P(None, "tensor"),
            P("tensor"),
            P("tensor", None),
            P(),
        ),
        check_vma=False,
    )
```
